128 devices in a mesh: kgrp: 4 (over z), vpair: 32 (over x, y, core).
Axes of the slice: x: 4, y: 4, z: 4, core: 2. Of those that a mesh axis runs over, the one named last changes fastest.
Arguments:
- amplitudes: bfloat16 [64, 2, 256, 4096], P('kgrp', None, None, 'vpair'), may hold values from -6 to 6
- ladder: bfloat16 [64, 2, 256, 256], P('kgrp'), may hold values from -0.25 to 0.25
- cycle: bfloat16 [4, 3, 2, 1024, 1024], P('kgrp'), may hold values from -0.078125 to 0.078125
- partner: int32 [64, 3], P('kgrp'), may hold values from 0 to 15
- occ_energy: float32 [64, 16], P('kgrp'), may hold values from -2 to -0.5
- vir_energy: float32 [64, 64], P('kgrp'), may hold values from 0.5 to 2.5
Outputs:
- updated: bfloat16 [64, 2, 256, 4096], P('kgrp', None, None, 'vpair')
The draws below stay inside these ranges and needn't reach their ends.
Inputs may be any that keep to these rules, and one draw needn't show every extreme that they name: The place of the partner block among the 16 blocks of its k-block group.
All inputs are finite; a program needn't handle non-finite values.
Results may differ from the reference program's by a relative error of at most 0.0049.
Values may be sent and summed in bfloat16 or wider, within the bound.
A program may use at most 192 MiB of HBM per device.

```python
import jax
import jax.numpy as jnp
from jax import lax

NO = 16
NV = 64
BLK = 16
TERMS = 3
GROUPS = 4
NB = 64
OO = 256
OV = 1024
VV = 4096


def with_ends(values, stream_key, low, top_value):
    longest = values.shape.index(max(values.shape))
    spots = []
    for shift in (0, 1):
        where = [jax.random.randint(jax.random.fold_in(stream_key, axis), (), 0, length) for axis, length in enumerate(values.shape)]
        where[longest] = (where[longest] + shift) % values.shape[longest]
        spots.append(tuple(where))
    return values.at[spots[0]].set(low).at[spots[1]].set(top_value)


def block_levels(rng, shape, split, low, high):
    def one(axis_at, shards_of):
        steps = jax.random.uniform(jax.random.fold_in(jax.random.fold_in(rng, 6), axis_at), (shards_of,), jnp.float32, low / len(split), high / len(split))
        return jnp.repeat(jnp.exp(steps), shape[axis_at] // shards_of).reshape((-1,) + (1,) * (len(shape) - axis_at - 1))

    level = one(*split[0])
    for cut in split[1:]:
        level = level * one(*cut)
    return level


def gaussian(rng, extent, width, bound, shards=(), held_as=jnp.bfloat16):
    level = block_levels(rng, extent, shards, -0.22, 0.18) if shards else 1.0
    values = jax.random.normal(rng, extent, jnp.float32) * width * level
    return jnp.minimum(jnp.maximum(values, -bound), bound).astype(held_as)


def setup_inputs(seed: int = 0) -> dict:
    streams_of = jax.random.split(jax.random.key(seed), 7)
    return {
        "amplitudes": gaussian(streams_of[0], (NB, 2, OO, VV), 1.0, 6.0, ((0, 4), (3, 32))),
        "ladder": gaussian(streams_of[1], (NB, 2, OO, OO), (2 * OO) ** -0.5, 0.25, ((0, 4),)),
        "cycle": gaussian(streams_of[2], (GROUPS, TERMS, 2, OV, OV), (2 * OV * TERMS) ** -0.5, 0.078125, ((0, 4),)),
        "partner": with_ends(jax.random.randint(streams_of[3], (NB, TERMS), 0, BLK), jax.random.fold_in(streams_of[3], 1), 0, BLK - 1).astype(jnp.int32),
        "occ_energy": jnp.clip(-2.0 + 1.5 * jax.random.uniform(streams_of[4], (NB, NO), jnp.float32) ** block_levels(streams_of[4], (NB, NO), ((0, 4),), -0.2, 0.2), -2.0, -0.5),
        "vir_energy": jnp.clip(0.5 + 2.0 * jax.random.uniform(streams_of[5], (NB, NV), jnp.float32) ** block_levels(streams_of[5], (NB, NV), ((0, 4),), -0.2, 0.2), 0.5, 2.5),
    }


def reference(amplitudes, ladder, cycle, partner, occ_energy, vir_energy):
    amp_float = amplitudes.astype(jnp.float32)
    ladder_float = ladder.astype(jnp.float32)
    real_part = jnp.einsum("nxy,nyz->nxz", ladder_float[:, 0], amp_float[:, 0]) - jnp.einsum("nxy,nyz->nxz", ladder_float[:, 1], amp_float[:, 1])
    imag_part = jnp.einsum("nxy,nyz->nxz", ladder_float[:, 0], amp_float[:, 1]) + jnp.einsum("nxy,nyz->nxz", ladder_float[:, 1], amp_float[:, 0])
    dressed = jnp.stack([real_part, imag_part], 1).astype(jnp.bfloat16)
    strips = dressed.reshape(NB, 2, NO, NO, NV, NV).transpose(0, 1, 5, 3, 2, 4).reshape(NB, 2, NV * NO, OV)
    offsets = jnp.array([0, 1, -1], dtype=jnp.int32)

    def one_block(block_id):
        group_id = block_id // BLK
        source_ids = (((group_id - offsets) % GROUPS) * BLK + partner[block_id]).astype(jnp.int32)
        selected = strips[source_ids].astype(jnp.float32)
        coupling = cycle[group_id].astype(jnp.float32)
        real_sum = jnp.einsum("qro,qoi->ri", selected[:, 0], coupling[:, 0]) - jnp.einsum("qro,qoi->ri", selected[:, 1], coupling[:, 1])
        imag_sum = jnp.einsum("qro,qoi->ri", selected[:, 0], coupling[:, 1]) + jnp.einsum("qro,qoi->ri", selected[:, 1], coupling[:, 0])
        return jnp.stack([real_sum, imag_sum], 0)

    cycle_sum = lax.map(one_block, jnp.arange(NB, dtype=jnp.int32))
    denominator = (vir_energy[:, :, None, None, None] + vir_energy[:, None, None, None, :]
                   - occ_energy[:, None, None, :, None] - occ_energy[:, None, :, None, None])
    numerator = strips.astype(jnp.float32) + cycle_sum
    result = (numerator.reshape(NB, 2, NV, NO, NO, NV) / denominator[:, None]).astype(jnp.bfloat16)
    return result.transpose(0, 1, 4, 3, 5, 2).reshape(NB, 2, OO, VV)
```

```python
import jax
import jax.numpy as jnp
from jax import lax
from jax.experimental import pallas as pl
from jax.experimental.pallas import tpu as pltpu
from jax.sharding import PartitionSpec as P

F32 = jnp.float32
BF16 = jnp.bfloat16
NT = (((1,), (1,)), ((), ()))
NN = (((1,), (0,)), ((), ()))
VMEM = pl.BlockSpec(memory_space=pltpu.VMEM)
SMEM = pl.BlockSpec(memory_space=pltpu.SMEM)


def shifted(value, axis, by):
    count = lax.axis_size(axis)
    return lax.ppermute(value, axis, [(i, (i + by) % count) for i in range(count)])


def permutations():
    row = lax.broadcasted_iota(jnp.int32, (1024, 1024), 0)
    col = lax.broadcasted_iota(jnp.int32, (1024, 1024), 1)
    x, r, n, y = row // 512, (row // 16) % 32, (row // 2) % 8, row % 2
    one = (col == n * 128 + y * 64 + r * 2 + x).astype(BF16)
    two = (col == n * 128 + x * 64 + r * 2 + y).astype(BF16)
    return one, two


def dress_kernel(t_ref, l_ref, p1_ref, out_ref, dcat):
    def per_block(n, _):
        group, place = n // 8, n % 8
        weights = jnp.concatenate((t_ref[n, 0], t_ref[n, 1]), axis=1)
        real = jnp.dot(l_ref[n, 0], weights, preferred_element_type=F32)
        imag = jnp.dot(l_ref[n, 1], weights, preferred_element_type=F32)
        lanes = pl.ds(pl.multiple_of(place * 128, 128), 128)
        parts = (real[:, :128] - imag[:, 128:], real[:, 128:] + imag[:, :128])
        for p in range(2):
            four = parts[p].astype(BF16).reshape(8, 2, 16, 128)
            for low in range(2):
                dcat[p, group, pl.ds(low * 128, 128), lanes] = four[:, low].reshape(128, 128)
        return 0

    lax.fori_loop(0, 16, per_block, 0)
    for p in range(2):
        for group in range(2):
            for quarter in range(4):
                moved = lax.dot_general(
                    p1_ref[pl.ds(quarter * 256, 256), :], dcat[p, group], NT, preferred_element_type=F32
                ).astype(BF16)
                parity = quarter // 2
                for r in range(16):
                    dest = (quarter % 2) * 16 + r
                    for low in range(2):
                        out_ref[dest, ((parity * 2 + p) * 2 + group) * 2 + low] = moved[
                            r * 16 : (r + 1) * 16, low * 128 : (low + 1) * 128
                        ]


def strip_kernel(x_ref, p2_ref, out_ref):
    for parity in range(2):
        for p in range(2):
            for group in range(2):
                index = ((parity * 2 + p) * 2 + group) * 2
                rows = jnp.concatenate(
                    [x_ref[:, index].reshape(512, 128), x_ref[:, index + 1].reshape(512, 128)], axis=0
                )
                moved = jnp.dot(rows.T, p2_ref[...], preferred_element_type=F32).astype(BF16)
                for place in range(8):
                    for k in range(8):
                        out_ref[parity, group * 8 + place, p, :, pl.ds(k * 128, 128)] = moved[
                            k * 16 : (k + 1) * 16, place * 128 : (place + 1) * 128
                        ]


def cycle_kernel(
    partner_ref, own_ref, low_ref, high_ref, w_ref, rows_ref, lanes_ref, p2_ref, out_ref, picked, regroup
):
    sources = (own_ref, low_ref, high_ref)
    for parity in range(2):
        for q in range(3):

            def pick(n, _):
                which = partner_ref[n, q]
                real = sources[q][parity, which, 0]
                imag = sources[q][parity, which, 1]
                near = pl.ds(pl.multiple_of(n * 16, 16), 16)
                far = pl.ds(pl.multiple_of(n * 16 + 256, 16), 16)
                picked[q, 0, near, :] = real
                picked[q, 0, far, :] = imag
                picked[q, 1, near, :] = -imag
                picked[q, 1, far, :] = real
                return 0

            lax.fori_loop(0, 16, pick, 0)

        def columns(step, _):
            span = pl.ds(pl.multiple_of(step * 256, 256), 256)
            total = jnp.zeros((512, 256), F32)
            for q in range(3):
                for part in range(2):
                    total += jnp.dot(picked[q, part], w_ref[q, part, :, span], preferred_element_type=F32)
            per_row = rows_ref[parity]
            per_lane = jnp.broadcast_to(lanes_ref[:, span][:, None, :], (16, 16, 256)).reshape(256, 256)
            scale = 1.0 / (per_row + per_lane)
            for p in range(2):
                strips = own_ref[parity, :, p, :, span].reshape(256, 256).astype(F32)
                result = ((strips + total[p * 256 : (p + 1) * 256]) * scale).astype(BF16)
                for n in range(16):
                    group, place = n // 8, n % 8
                    for half in range(2):
                        rows = pl.ds(pl.multiple_of(group * 128 + step * 32 + half * 16, 16), 16)
                        regroup[p, rows, pl.ds(place * 128, 128)] = result[
                            n * 16 : (n + 1) * 16, half * 128 : (half + 1) * 128
                        ]
            return 0

        lax.fori_loop(0, 4, columns, 0)
        for p in range(2):
            for quarter in range(4):
                moved = lax.dot_general(
                    p2_ref[pl.ds(quarter * 256, 256), :], regroup[p], NT, preferred_element_type=F32
                ).astype(BF16)
                low = quarter // 2
                for r in range(16):
                    dest = (quarter % 2) * 16 + r
                    for group in range(2):
                        out_ref[dest, ((parity * 2 + p) * 2 + group) * 2 + low] = moved[
                            r * 16 : (r + 1) * 16, group * 128 : (group + 1) * 128
                        ]


def final_kernel(y_ref, p1_ref, out_ref):
    for p in range(2):
        for group in range(2):
            for low in range(2):
                rows = jnp.concatenate(
                    [
                        y_ref[:, ((parity * 2 + p) * 2 + group) * 2 + low].reshape(512, 128)
                        for parity in range(2)
                    ],
                    axis=0,
                )
                moved = jnp.dot(rows.T, p1_ref[...], preferred_element_type=F32).astype(BF16)
                for place in range(8):
                    for i in range(8):
                        out_ref[group * 8 + place, p, pl.ds((i * 2 + low) * 16, 16), :] = moved[
                            i * 16 : (i + 1) * 16, place * 128 : (place + 1) * 128
                        ]


def call(kernel, shape, specs, args, scratch=()):
    return pl.pallas_call(
        kernel,
        out_shape=jax.ShapeDtypeStruct(shape, BF16),
        in_specs=specs,
        out_specs=VMEM,
        scratch_shapes=scratch,
        compiler_params=pltpu.CompilerParams(vmem_limit_bytes=56 * 1024 * 1024),
    )(*args)


def per_device(amplitudes, ladder, cycle, partner, occ_energy, vir_energy):
    one, two = permutations()
    sent = call(
        dress_kernel,
        (32, 16, 16, 128),
        [VMEM] * 3,
        (amplitudes, ladder, one),
        [pltpu.VMEM((2, 2, 256, 1024), BF16)],
    )
    arrived = lax.all_to_all(sent, "vpair", split_axis=0, concat_axis=0, tiled=True)
    strips = call(strip_kernel, (2, 16, 2, 16, 1024), [VMEM] * 2, (arrived, two))
    from_lower = shifted(strips, "kgrp", 1)
    from_upper = shifted(strips, "kgrp", -1)
    rank = lax.axis_index("vpair")
    own = lax.dynamic_slice_in_dim(vir_energy, rank * 2, 2, 1)
    rows = (own.T[:, :, None] - occ_energy[None]).reshape(2, 256, 1)
    lanes = (vir_energy[:, None, :] - occ_energy[:, :, None]).reshape(16, 1024)
    sent = call(
        cycle_kernel,
        (32, 16, 16, 128),
        [SMEM] + [VMEM] * 7,
        (partner, strips, from_lower, from_upper, cycle[0], rows, lanes, two),
        [pltpu.VMEM((3, 2, 512, 1024), BF16), pltpu.VMEM((2, 256, 1024), BF16)],
    )
    arrived = lax.all_to_all(sent, "vpair", split_axis=0, concat_axis=0, tiled=True)
    return call(final_kernel, (16, 2, 256, 128), [VMEM] * 2, (arrived, one))


def solution(mesh):
    return jax.shard_map(
        per_device,
        mesh=mesh,
        in_specs=(
            P("kgrp", None, None, "vpair"),
            P("kgrp", None, None, None),
            P("kgrp", None, None, None, None),
            P("kgrp", None),
            P("kgrp", None),
            P("kgrp", None),
        ),
        out_specs=P("kgrp", None, None, "vpair"),
        check_vma=False,
    )
```

```python
import jax
import jax.numpy as jnp
from jax import lax
from jax.experimental import pallas as pl
from jax.experimental.pallas import tpu as pltpu
from jax.sharding import PartitionSpec as P

F32 = jnp.float32
BF16 = jnp.bfloat16
NT = (((1,), (1,)), ((), ()))
MESH = pl.DeviceIdType.MESH
RANKS = 32


def permutation(ref, swapped):
    def block(step, _):
        row = lax.broadcasted_iota(jnp.int32, (64, 1024), 0) + step * 64
        col = lax.broadcasted_iota(jnp.int32, (64, 1024), 1)
        x, r, n, y = row >> 9, (row >> 4) & 31, (row >> 1) & 7, row & 1
        if swapped:
            x, y = y, x
        target = n * 128 + x * 64 + r * 2 + y
        ref[pl.ds(pl.multiple_of(step * 64, 64), 64), :] = jnp.where(col == target, 1.0, 0.0).astype(BF16)
        return 0

    lax.fori_loop(0, 16, block, 0)


def kernel(
    t_hbm,
    l_hbm,
    w_hbm,
    partner,
    occ,
    vir,
    vir_rows,
    out,
    t_ref,
    l_ref,
    w_ref,
    one,
    two,
    dcat,
    send1,
    x_ref,
    strips_even,
    strips_odd,
    low_even,
    low_odd,
    high_even,
    high_odd,
    picked,
    total,
    scale,
    regroup,
    send2,
    y_ref,
    load_sem,
    send1_sem,
    recv1_sem,
    shift_send_sem,
    shift_recv_sem,
    send2_sem,
    recv2_sem,
):
    group = lax.axis_index("kgrp")
    me = lax.axis_index("vpair")
    above, below = lax.rem(group + 1, 4), lax.rem(group + 3, 4)
    strips, low_ref, high_ref = (strips_even, strips_odd), (low_even, low_odd), (high_even, high_odd)

    loads = []
    for half in range(2):
        span = pl.ds(half * 8, 8)
        loads.append(
            (
                pltpu.make_async_copy(t_hbm.at[span], t_ref.at[span], load_sem.at[2 * half]),
                pltpu.make_async_copy(l_hbm.at[span], l_ref.at[span], load_sem.at[2 * half + 1]),
            )
        )
    w_load = pltpu.make_async_copy(w_hbm, w_ref, load_sem.at[4])
    for pair in loads:
        for copy in pair:
            copy.start()
    w_load.start()

    barrier = pltpu.get_barrier_semaphore()

    def greet(i, _):
        pl.semaphore_signal(barrier, inc=1, device_id=(group, lax.rem(me + i, RANKS)), device_id_type=MESH)
        return 0

    lax.fori_loop(1, RANKS, greet, 0)
    for other in (above, below):
        pl.semaphore_signal(barrier, inc=1, device_id=(other, me), device_id_type=MESH)

    mine = pl.ds(pl.multiple_of(me * 16, 16), 16)

    def spread(source, target, send_sem, recv_sem):
        def one_peer(i, _):
            peer = lax.rem(me + i, RANKS)
            pltpu.make_async_remote_copy(
                src_ref=source.at[:, :, pl.ds(pl.multiple_of(peer * 16, 16), 16), :],
                dst_ref=target.at[:, :, mine, :],
                send_sem=send_sem,
                recv_sem=recv_sem,
                device_id=(group, peer),
                device_id_type=MESH,
            ).start()
            return 0

        lax.fori_loop(1, RANKS, one_peer, 0)

    def await_peers(ref, sem):
        part = ref.at[:, :, pl.ds(0, 16 * (RANKS - 1)), :]
        pltpu.make_async_copy(part, part, sem).wait()

    def dress(half):
        def per_block(place, _):
            n = half * 8 + place
            weights = jnp.concatenate((t_ref[n, 0], t_ref[n, 1]), axis=1)
            real = jnp.dot(l_ref[n, 0], weights, preferred_element_type=F32)
            imag = jnp.dot(l_ref[n, 1], weights, preferred_element_type=F32)
            lanes = pl.ds(pl.multiple_of(place * 128, 128), 128)
            parts = (real[:, :128] - imag[:, 128:], real[:, 128:] + imag[:, :128])
            for p in range(2):
                four = parts[p].astype(BF16).reshape(8, 2, 16, 128)
                for low in range(2):
                    dcat[p, half, pl.ds(low * 128, 128), lanes] = four[:, low].reshape(128, 128)
            return 0

        lax.fori_loop(0, 8, per_block, 0)

    def spread_dressed(parity, half):
        for p in range(2):
            for part in range(2):
                moved = lax.dot_general(
                    one[pl.ds(parity * 512 + part * 256, 256), :],
                    dcat[p, half],
                    NT,
                    preferred_element_type=F32,
                ).astype(BF16)
                for low in range(2):
                    send1[parity, half, p, low, pl.ds(part * 256, 256), :] = moved[:, low * 128 : (low + 1) * 128]
        x_ref[parity, half, :, :, mine, :] = send1[parity, half, :, :, mine, :]
        spread(send1.at[parity, half], x_ref.at[parity, half], send1_sem.at[parity, half], recv1_sem.at[parity, half])

    def shifts(parity, half):
        piece = strips[parity].at[pl.ds(half * 8, 8)]
        return [
            pltpu.make_async_remote_copy(
                src_ref=piece,
                dst_ref=target[parity].at[pl.ds(half * 8, 8)],
                send_sem=shift_send_sem.at[way, parity, half],
                recv_sem=shift_recv_sem.at[way, parity, half],
                device_id=(other, me),
                device_id_type=MESH,
            )
            for way, (target, other) in enumerate(((low_ref, above), (high_ref, below)))
        ]

    def make_strips(parity, half):
        await_peers(x_ref.at[parity, half], recv1_sem.at[parity, half])
        rows = jnp.concatenate([x_ref[parity, half, p].reshape(1024, 128).T for p in range(2)], axis=0)
        moved = jnp.dot(rows, two[...], preferred_element_type=F32).astype(BF16)
        for place in range(8):
            for p in range(2):
                for k in range(8):
                    strips[parity][half * 8 + place, p, :, pl.ds(k * 128, 128)] = moved[
                        p * 128 + k * 16 : p * 128 + (k + 1) * 16, place * 128 : (place + 1) * 128
                    ]
        for copy in shifts(parity, half):
            copy.start()

    def make_scale(parity):
        def per_block(n, _):
            row = lax.broadcasted_iota(jnp.int32, (16, 128), 0)
            lane = lax.broadcasted_iota(jnp.int32, (16, 128), 1)
            own = vir[n, 2 * me + parity]
            per_row = jnp.zeros((16, 128), F32)
            for j in range(16):
                per_row = jnp.where(row == j, own - occ[n, j], per_row)
            both = vir_rows[pl.ds(n, 1), :]
            both = jnp.broadcast_to(jnp.concatenate((both, both), axis=1), (16, 128))
            rows = pl.ds(pl.multiple_of(n * 16, 16), 16)
            for pair in range(8):
                per_lane = both - jnp.where(lane < 64, occ[n, 2 * pair], occ[n, 2 * pair + 1])
                scale[rows, pl.ds(pair * 128, 128)] = 1.0 / (per_row + per_lane)
            return 0

        lax.fori_loop(0, 16, per_block, 0)

    def pick(parity, q, source):
        def per_block(n, _):
            which = partner[n, q]
            real = source[parity][which, 0]
            imag = source[parity][which, 1]
            near = pl.ds(pl.multiple_of(n * 16, 16), 16)
            far = pl.ds(pl.multiple_of(n * 16 + 256, 16), 16)
            picked[q, 0, near, :] = real
            picked[q, 0, far, :] = imag
            picked[q, 1, near, :] = -imag
            picked[q, 1, far, :] = real
            return 0

        lax.fori_loop(0, 16, per_block, 0)

    def own_cycle(parity):
        pick(parity, 0, strips)

        def columns(step, _):
            span = pl.ds(pl.multiple_of(step * 256, 256), 256)
            some = jnp.dot(picked[0, 0], w_ref[0, 0, :, span], preferred_element_type=F32)
            some += jnp.dot(picked[0, 1], w_ref[0, 1, :, span], preferred_element_type=F32)
            for p in range(2):
                total[pl.ds(p * 256, 256), span] = some[p * 256 : (p + 1) * 256] + strips[parity][
                    :, p, :, span
                ].reshape(256, 256).astype(F32)
            return 0

        lax.fori_loop(0, 4, columns, 0)
        make_scale(parity)

    def far_cycle(parity):
        for half in range(2):
            for copy in shifts(parity, half):
                copy.wait_recv()
        pick(parity, 1, low_ref)
        pick(parity, 2, high_ref)

        def columns(step, _):
            span = pl.ds(pl.multiple_of(step * 256, 256), 256)
            some = total[:, span]
            for q in (1, 2):
                for part in range(2):
                    some += jnp.dot(picked[q, part], w_ref[q, part, :, span], preferred_element_type=F32)
            for p in range(2):
                result = (some[p * 256 : (p + 1) * 256] * scale[:, span]).astype(BF16)
                for n in range(16):
                    half, place = n // 8, n % 8
                    for pair in range(2):
                        rows = pl.ds(pl.multiple_of(half * 128 + step * 32 + pair * 16, 16), 16)
                        regroup[p, rows, pl.ds(place * 128, 128)] = result[
                            n * 16 : (n + 1) * 16, pair * 128 : (pair + 1) * 128
                        ]
            return 0

        lax.fori_loop(0, 4, columns, 0)
        for p in range(2):
            for part in range(4):
                moved = lax.dot_general(
                    two[pl.ds(part * 256, 256), :], regroup[p], NT, preferred_element_type=F32
                ).astype(BF16)
                for half in range(2):
                    send2[parity, p, half, part // 2, pl.ds((part % 2) * 256, 256), :] = moved[
                        :, half * 128 : (half + 1) * 128
                    ]
            y_ref[parity, p, :, :, mine, :] = send2[parity, p, :, :, mine, :]
            spread(send2.at[parity, p], y_ref.at[parity, p], send2_sem.at[parity, p], recv2_sem.at[parity, p])

    def finish(parity, p):
        await_peers(y_ref.at[parity, p], recv2_sem.at[parity, p])
        for half in range(2):
            rows = jnp.concatenate([y_ref[parity, p, half, low].T for low in range(2)], axis=0)
            moved = jnp.dot(rows, one[pl.ds(parity * 512, 512), :], preferred_element_type=F32).astype(BF16)
            for place in range(8):
                for low in range(2):
                    for i in range(8):
                        where = (half * 8 + place, p, pl.ds((i * 2 + low) * 16, 16))
                        tile = moved[
                            low * 128 + i * 16 : low * 128 + (i + 1) * 16, place * 128 : (place + 1) * 128
                        ]
                        if parity == 0:
                            out[where] = tile
                        else:
                            out[where] = out[where] + tile

    permutation(one, True)
    for copy in loads[0]:
        copy.wait()
    dress(0)
    pl.semaphore_wait(barrier, RANKS + 1)
    spread_dressed(0, 0)
    for copy in loads[1]:
        copy.wait()
    dress(1)
    spread_dressed(0, 1)
    spread_dressed(1, 0)
    spread_dressed(1, 1)
    permutation(two, False)
    make_strips(0, 0)
    make_strips(0, 1)
    w_load.wait()
    own_cycle(0)
    make_strips(1, 0)
    make_strips(1, 1)
    far_cycle(0)
    own_cycle(1)
    far_cycle(1)
    for parity in range(2):
        for p in range(2):
            finish(parity, p)
    for parity in range(2):
        for half in range(2):
            await_peers(send1.at[parity, half], send1_sem.at[parity, half])
            await_peers(send2.at[parity, half], send2_sem.at[parity, half])
            for copy in shifts(parity, half):
                copy.wait_send()


def per_device(amplitudes, ladder, cycle, partner, occ_energy, vir_energy):
    hbm = pl.BlockSpec(memory_space=pl.ANY)
    smem = pl.BlockSpec(memory_space=pltpu.SMEM)
    vmem = pl.BlockSpec(memory_space=pltpu.VMEM)
    exchanged = pltpu.VMEM((2, 2, 2, 2, 512, 128), BF16)
    field = pltpu.VMEM((16, 2, 16, 1024), BF16)
    square = pltpu.VMEM((1024, 1024), BF16)
    dma = pltpu.SemaphoreType.DMA
    return pl.pallas_call(
        kernel,
        out_shape=jax.ShapeDtypeStruct((16, 2, 256, 128), BF16),
        in_specs=[hbm, hbm, hbm, smem, smem, smem, vmem],
        out_specs=vmem,
        scratch_shapes=[
            pltpu.VMEM((16, 2, 256, 128), BF16),
            pltpu.VMEM((16, 2, 256, 256), BF16),
            pltpu.VMEM((3, 2, 1024, 1024), BF16),
            square,
            square,
            pltpu.VMEM((2, 2, 256, 1024), BF16),
            exchanged,
            exchanged,
            field,
            field,
            field,
            field,
            field,
            field,
            pltpu.VMEM((3, 2, 512, 1024), BF16),
            pltpu.VMEM((512, 1024), F32),
            pltpu.VMEM((256, 1024), F32),
            pltpu.VMEM((2, 256, 1024), BF16),
            exchanged,
            exchanged,
            dma((5,)),
            dma((2, 2)),
            dma((2, 2)),
            dma((2, 2, 2)),
            dma((2, 2, 2)),
            dma((2, 2)),
            dma((2, 2)),
        ],
        compiler_params=pltpu.CompilerParams(
            collective_id=0, has_side_effects=True, vmem_limit_bytes=60 * 1024 * 1024
        ),
    )(amplitudes, ladder, cycle[0], partner, occ_energy, vir_energy, vir_energy)


def solution(mesh):
    return jax.shard_map(
        per_device,
        mesh=mesh,
        in_specs=(
            P("kgrp", None, None, "vpair"),
            P("kgrp", None, None, None),
            P("kgrp", None, None, None, None),
            P("kgrp", None),
            P("kgrp", None),
            P("kgrp", None),
        ),
        out_specs=P("kgrp", None, None, "vpair"),
        check_vma=False,
    )
```

```python
import jax
import jax.numpy as jnp
from jax import lax
from jax.experimental import pallas as pl
from jax.experimental.pallas import tpu as pltpu
from jax.sharding import PartitionSpec as P

F32 = jnp.float32
BF16 = jnp.bfloat16
NT = (((1,), (1,)), ((), ()))
MESH = pl.DeviceIdType.MESH
RANKS = 32


def permutation(ref, swapped):
    def block(step, _):
        row = lax.broadcasted_iota(jnp.int32, (64, 1024), 0) + step * 64
        col = lax.broadcasted_iota(jnp.int32, (64, 1024), 1)
        x, r, n, y = row >> 9, (row >> 4) & 31, (row >> 1) & 7, row & 1
        if swapped:
            x, y = y, x
        target = n * 128 + x * 64 + r * 2 + y
        ref[pl.ds(pl.multiple_of(step * 64, 64), 64), :] = jnp.where(col == target, 1.0, 0.0).astype(BF16)
        return 0

    lax.fori_loop(0, 16, block, 0)


def kernel(
    t_hbm,
    l_hbm,
    w_hbm,
    partner,
    occ,
    vir,
    vir_rows,
    out,
    t_ref,
    l_ref,
    w_ref,
    one,
    two,
    dcat,
    send1,
    x_ref,
    *rest,
):
    strips, low_ref, high_ref = rest[:4], rest[4:8], rest[8:12]
    (
        picked,
        total,
        scale,
        regroup,
        send2,
        y_ref,
        load_sem,
        send1_sem,
        recv1_sem,
        shift_send_sem,
        shift_recv_sem,
        send2_sem,
        recv2_sem,
    ) = rest[12:]
    group = lax.axis_index("kgrp")
    me = lax.axis_index("vpair")
    above, below = lax.rem(group + 1, 4), lax.rem(group + 3, 4)

    loads = []
    for half in range(2):
        span = pl.ds(half * 8, 8)
        loads.append(
            (
                pltpu.make_async_copy(t_hbm.at[span], t_ref.at[span], load_sem.at[2 * half]),
                pltpu.make_async_copy(l_hbm.at[span], l_ref.at[span], load_sem.at[2 * half + 1]),
            )
        )
    w_load = pltpu.make_async_copy(w_hbm, w_ref, load_sem.at[4])
    for pair in loads:
        for copy in pair:
            copy.start()
    w_load.start()

    barrier = pltpu.get_barrier_semaphore()

    def greet(i, _):
        pl.semaphore_signal(barrier, inc=1, device_id=(group, lax.rem(me + i, RANKS)), device_id_type=MESH)
        return 0

    lax.fori_loop(1, RANKS, greet, 0)
    for other in (above, below):
        pl.semaphore_signal(barrier, inc=1, device_id=(other, me), device_id_type=MESH)

    mine = pl.ds(pl.multiple_of(me * 16, 16), 16)

    def spread(source, target, send_sem, recv_sem):
        def one_peer(i, _):
            peer = lax.rem(me + i, RANKS)
            pltpu.make_async_remote_copy(
                src_ref=source.at[:, :, pl.ds(pl.multiple_of(peer * 16, 16), 16), :],
                dst_ref=target.at[:, :, mine, :],
                send_sem=send_sem,
                recv_sem=recv_sem,
                device_id=(group, peer),
                device_id_type=MESH,
            ).start()
            return 0

        lax.fori_loop(1, RANKS, one_peer, 0)

    def await_peers(ref, sem):
        part = ref.at[:, :, pl.ds(0, 16 * (RANKS - 1)), :]
        pltpu.make_async_copy(part, part, sem).wait()

    def dress(half):
        def per_block(place, _):
            n = half * 8 + place
            weights = jnp.concatenate((t_ref[n, 0], t_ref[n, 1]), axis=1)
            real = jnp.dot(l_ref[n, 0], weights, preferred_element_type=F32)
            imag = jnp.dot(l_ref[n, 1], weights, preferred_element_type=F32)
            lanes = pl.ds(pl.multiple_of(place * 128, 128), 128)
            parts = (real[:, :128] - imag[:, 128:], real[:, 128:] + imag[:, :128])
            parts = [part.reshape(8, 2, 2, 8, 128) for part in parts]
            for side in range(2):
                for low in range(2):
                    both = jnp.stack([part[:, low, side] for part in parts], axis=1)
                    dcat[side, half, pl.ds(low * 128, 128), lanes] = both.reshape(128, 128).astype(BF16)
            return 0

        lax.fori_loop(0, 8, per_block, 0)

    def spread_dressed(parity, half):
        for side in range(2):
            for part in range(2):
                moved = lax.dot_general(
                    one[pl.ds(parity * 512 + part * 256, 256), :],
                    dcat[side, half],
                    NT,
                    preferred_element_type=F32,
                ).astype(BF16)
                for low in range(2):
                    send1[parity, half, side, low, pl.ds(part * 256, 256), :] = moved[:, low * 128 : (low + 1) * 128]
        x_ref[parity, half, :, :, mine, :] = send1[parity, half, :, :, mine, :]
        spread(send1.at[parity, half], x_ref.at[parity, half], send1_sem.at[parity, half], recv1_sem.at[parity, half])

    def shifts(chunk, half):
        piece = pl.ds(half * 8, 8)
        return [
            pltpu.make_async_remote_copy(
                src_ref=strips[chunk].at[piece],
                dst_ref=target[chunk].at[piece],
                send_sem=shift_send_sem.at[way, chunk, half],
                recv_sem=shift_recv_sem.at[way, chunk, half],
                device_id=(other, me),
                device_id_type=MESH,
            )
            for way, (target, other) in enumerate(((low_ref, above), (high_ref, below)))
        ]

    def start_shifts(chunk, half):
        for copy in shifts(chunk, half):
            copy.start()

    def make_strips(parity, half):
        await_peers(x_ref.at[parity, half], recv1_sem.at[parity, half])
        rows = jnp.concatenate([x_ref[parity, half, side].reshape(1024, 128).T for side in range(2)], axis=0)
        moved = jnp.dot(rows, two[...], preferred_element_type=F32).astype(BF16)
        for side in range(2):
            for place in range(8):
                for k in range(8):
                    strips[2 * parity + side][half * 8 + place, :, pl.ds(k * 128, 128)] = moved[
                        side * 128 + k * 16 : side * 128 + (k + 1) * 16, place * 128 : (place + 1) * 128
                    ]

    def make_scale(chunk):
        parity, side = chunk // 2, chunk % 2

        def per_block(n, _):
            row = lax.broadcasted_iota(jnp.int32, (8, 128), 0)
            lane = lax.broadcasted_iota(jnp.int32, (8, 128), 1)
            own = vir[n, 2 * me + parity]
            per_row = jnp.zeros((8, 128), F32)
            for j in range(8):
                per_row = jnp.where(row == j, own - occ[n, side * 8 + j], per_row)
            both = vir_rows[pl.ds(n, 1), :]
            both = jnp.broadcast_to(jnp.concatenate((both, both), axis=1), (8, 128))
            for pair in range(8):
                per_lane = both - jnp.where(lane < 64, occ[n, 2 * pair], occ[n, 2 * pair + 1])
                scale[n, :, pl.ds(pair * 128, 128)] = 1.0 / (per_row + per_lane)
            return 0

        lax.fori_loop(0, 16, per_block, 0)

    def pick(chunk, q, source):
        def per_block(n, _):
            picked[q, pl.ds(pl.multiple_of(n * 16, 16), 16), :] = source[chunk][partner[q, n]]
            return 0

        lax.fori_loop(0, 16, per_block, 0)

    def own_cycle(chunk):
        pick(chunk, 0, strips)

        def columns(step, _):
            span = pl.ds(pl.multiple_of(step * 256, 256), 256)
            for part in range(2):
                total[part, :, span] = jnp.dot(picked[0], w_ref[0, part, :, span], preferred_element_type=F32)
            return 0

        lax.fori_loop(0, 4, columns, 0)
        make_scale(chunk)

    def far_cycle(chunk):
        for half in range(2):
            for copy in shifts(chunk, half):
                copy.wait_recv()
        pick(chunk, 1, low_ref)
        pick(chunk, 2, high_ref)
        parity, side = chunk // 2, chunk % 2

        def columns(step, _):
            span = pl.ds(pl.multiple_of(step * 256, 256), 256)
            sums = []
            for part in range(2):
                some = total[part, :, span]
                for q in (1, 2):
                    some += jnp.dot(picked[q], w_ref[q, part, :, span], preferred_element_type=F32)
                sums.append(some.reshape(16, 2, 8, 256))
            by_real, by_imag = sums
            held = strips[chunk][:, :, span].astype(F32).reshape(16, 2, 8, 256)
            factor = scale[:, :, span]
            real = (held[:, 0] + (by_real[:, 0] - by_imag[:, 1])) * factor
            imag = (held[:, 1] + (by_imag[:, 0] + by_real[:, 1])) * factor
            result = jnp.stack((real, imag), axis=1).reshape(256, 256).astype(BF16)
            for n in range(16):
                half, place = n // 8, n % 8
                for pair in range(2):
                    rows = pl.ds(pl.multiple_of(half * 128 + step * 32 + pair * 16, 16), 16)
                    regroup[rows, pl.ds(place * 128, 128)] = result[
                        n * 16 : (n + 1) * 16, pair * 128 : (pair + 1) * 128
                    ]
            return 0

        lax.fori_loop(0, 4, columns, 0)
        for part in range(4):
            moved = lax.dot_general(
                two[pl.ds(part * 256, 256), :], regroup[...], NT, preferred_element_type=F32
            ).astype(BF16)
            for half in range(2):
                send2[parity, side, half, part // 2, pl.ds((part % 2) * 256, 256), :] = moved[
                    :, half * 128 : (half + 1) * 128
                ]
        y_ref[parity, side, :, :, mine, :] = send2[parity, side, :, :, mine, :]
        spread(send2.at[parity, side], y_ref.at[parity, side], send2_sem.at[parity, side], recv2_sem.at[parity, side])

    def unpacked(chunk, half):
        parity, side = chunk // 2, chunk % 2
        rows = jnp.concatenate([y_ref[parity, side, half, low].T for low in range(2)], axis=0)
        moved = jnp.dot(rows, one[pl.ds(parity * 512, 512), :], preferred_element_type=F32)
        return moved.reshape(2, 8, 2, 8, 1024)

    def finish(chunks):
        for chunk in chunks:
            where = chunk // 2, chunk % 2
            await_peers(y_ref.at[where], recv2_sem.at[where])
        for half in range(2):
            known = {chunk % 2: unpacked(chunk, half) for chunk in chunks}
            for place in range(8):
                for low in range(2):
                    for i in range(8):
                        for p in range(2):
                            tiles = [
                                known[side][low, i, p, :, place * 128 : (place + 1) * 128]
                                if side in known
                                else jnp.zeros((8, 128), F32)
                                for side in range(2)
                            ]
                            tile = jnp.concatenate(tiles, axis=0).astype(BF16)
                            spot = (half * 8 + place, p, pl.ds((i * 2 + low) * 16, 16))
                            out[spot] = tile if chunks[0] < 2 else out[spot] + tile

    permutation(one, True)
    for copy in loads[0]:
        copy.wait()
    dress(0)
    pl.semaphore_wait(barrier, RANKS + 1)
    spread_dressed(0, 0)
    for copy in loads[1]:
        copy.wait()
    dress(1)
    spread_dressed(0, 1)
    spread_dressed(1, 0)
    spread_dressed(1, 1)
    permutation(two, False)
    make_strips(0, 0)
    start_shifts(0, 0)
    make_strips(0, 1)
    start_shifts(0, 1)
    start_shifts(1, 0)
    start_shifts(1, 1)
    w_load.wait()
    own_cycle(0)
    make_strips(1, 0)
    make_strips(1, 1)
    for chunk in (2, 3):
        for half in range(2):
            start_shifts(chunk, half)
    far_cycle(0)
    own_cycle(1)
    far_cycle(1)
    own_cycle(2)
    far_cycle(2)
    own_cycle(3)
    finish((0, 1))
    far_cycle(3)
    finish((2,))
    finish((3,))
    for first in range(2):
        for second in range(2):
            await_peers(send1.at[first, second], send1_sem.at[first, second])
            await_peers(send2.at[first, second], send2_sem.at[first, second])
    for chunk in range(4):
        for half in range(2):
            for copy in shifts(chunk, half):
                copy.wait_send()


def per_device(amplitudes, ladder, cycle, partner, occ_energy, vir_energy):
    hbm = pl.BlockSpec(memory_space=pl.ANY)
    smem = pl.BlockSpec(memory_space=pltpu.SMEM)
    vmem = pl.BlockSpec(memory_space=pltpu.VMEM)
    exchanged = pltpu.VMEM((2, 2, 2, 2, 512, 128), BF16)
    field = pltpu.VMEM((16, 16, 1024), BF16)
    square = pltpu.VMEM((1024, 1024), BF16)
    dma = pltpu.SemaphoreType.DMA
    return pl.pallas_call(
        kernel,
        out_shape=jax.ShapeDtypeStruct((16, 2, 256, 128), BF16),
        in_specs=[hbm, hbm, hbm, smem, smem, smem, vmem],
        out_specs=vmem,
        scratch_shapes=[
            pltpu.VMEM((16, 2, 256, 128), BF16),
            pltpu.VMEM((16, 2, 256, 256), BF16),
            pltpu.VMEM((3, 2, 1024, 1024), BF16),
            square,
            square,
            pltpu.VMEM((2, 2, 256, 1024), BF16),
            exchanged,
            exchanged,
            *[field] * 12,
            pltpu.VMEM((3, 256, 1024), BF16),
            pltpu.VMEM((2, 256, 1024), F32),
            pltpu.VMEM((16, 8, 1024), F32),
            pltpu.VMEM((256, 1024), BF16),
            exchanged,
            exchanged,
            dma((5,)),
            dma((2, 2)),
            dma((2, 2)),
            dma((2, 4, 2)),
            dma((2, 4, 2)),
            dma((2, 2)),
            dma((2, 2)),
        ],
        compiler_params=pltpu.CompilerParams(
            collective_id=0, has_side_effects=True, vmem_limit_bytes=60 * 1024 * 1024
        ),
    )(amplitudes, ladder, cycle[0], partner.T, occ_energy, vir_energy, vir_energy)


def solution(mesh):
    return jax.shard_map(
        per_device,
        mesh=mesh,
        in_specs=(
            P("kgrp", None, None, "vpair"),
            P("kgrp", None, None, None),
            P("kgrp", None, None, None, None),
            P("kgrp", None),
            P("kgrp", None),
            P("kgrp", None),
        ),
        out_specs=P("kgrp", None, None, "vpair"),
        check_vma=False,
    )
```

```python
import jax
import jax.numpy as jnp
from jax import lax
from jax.experimental import pallas as pl
from jax.experimental.pallas import tpu as pltpu
from jax.sharding import PartitionSpec as P

F32 = jnp.float32
BF16 = jnp.bfloat16
NT = (((1,), (1,)), ((), ()))
MESH = pl.DeviceIdType.MESH
RANKS = 32


def permutation(ref, swapped):
    def block(step, _):
        row = lax.broadcasted_iota(jnp.int32, (64, 1024), 0) + step * 64
        col = lax.broadcasted_iota(jnp.int32, (64, 1024), 1)
        x, r, n, y = row >> 9, (row >> 4) & 31, (row >> 1) & 7, row & 1
        if swapped:
            x, y = y, x
        target = n * 128 + x * 64 + r * 2 + y
        ref[pl.ds(pl.multiple_of(step * 64, 64), 64), :] = jnp.where(col == target, 1.0, 0.0).astype(BF16)
        return 0

    lax.fori_loop(0, 16, block, 0)


def kernel(
    t_hbm,
    l_hbm,
    w_hbm,
    partner,
    occ,
    vir,
    vir_rows,
    out_hbm,
    t_ref,
    l_ref,
    w_ref,
    one,
    two,
    dcat,
    send1,
    x_ref,
    *rest,
):
    strips, low_ref, high_ref = rest[:4], rest[4:8], rest[8:12]
    (
        picked,
        total,
        scale,
        regroup,
        out,
        send2,
        y_ref,
        load_sem,
        send1_sem,
        recv1_sem,
        shift_send_sem,
        shift_recv_sem,
        send2_sem,
        recv2_sem,
    ) = rest[12:]
    group = lax.axis_index("kgrp")
    me = lax.axis_index("vpair")
    above, below = lax.rem(group + 1, 4), lax.rem(group + 3, 4)

    loads = []
    for half in range(2):
        span = pl.ds(half * 8, 8)
        loads.append(
            (
                pltpu.make_async_copy(t_hbm.at[span], t_ref.at[span], load_sem.at[2 * half]),
                pltpu.make_async_copy(l_hbm.at[span], l_ref.at[span], load_sem.at[2 * half + 1]),
            )
        )
    w_load = pltpu.make_async_copy(w_hbm, w_ref, load_sem.at[4])
    for pair in loads:
        for copy in pair:
            copy.start()
    w_load.start()

    barrier = pltpu.get_barrier_semaphore()

    def greet(i, _):
        pl.semaphore_signal(barrier, inc=1, device_id=(group, lax.rem(me + i, RANKS)), device_id_type=MESH)
        return 0

    lax.fori_loop(1, RANKS, greet, 0)
    for other in (above, below):
        pl.semaphore_signal(barrier, inc=1, device_id=(other, me), device_id_type=MESH)

    mine = pl.ds(pl.multiple_of(me * 16, 16), 16)

    def spread(source, target, send_sem, recv_sem):
        ahead = (slice(None),) * (len(source.shape) - 2)

        def one_peer(i, _):
            peer = lax.rem(me + i, RANKS)
            pltpu.make_async_remote_copy(
                src_ref=source.at[(*ahead, pl.ds(pl.multiple_of(peer * 16, 16), 16), slice(None))],
                dst_ref=target.at[(*ahead, mine, slice(None))],
                send_sem=send_sem,
                recv_sem=recv_sem,
                device_id=(group, peer),
                device_id_type=MESH,
            ).start()
            return 0

        lax.fori_loop(1, RANKS, one_peer, 0)

    def await_peers(ref, sem):
        ahead = (slice(None),) * (len(ref.shape) - 2)
        part = ref.at[(*ahead, pl.ds(0, 16 * (RANKS - 1)), slice(None))]
        pltpu.make_async_copy(part, part, sem).wait()

    def dress(half):
        def per_block(place, _):
            n = half * 8 + place
            weights = jnp.concatenate((t_ref[n, 0], t_ref[n, 1]), axis=1)
            real = jnp.dot(l_ref[n, 0], weights, preferred_element_type=F32)
            imag = jnp.dot(l_ref[n, 1], weights, preferred_element_type=F32)
            lanes = pl.ds(pl.multiple_of(place * 128, 128), 128)
            parts = (real[:, :128] - imag[:, 128:], real[:, 128:] + imag[:, :128])
            parts = [part.reshape(8, 2, 2, 8, 128) for part in parts]
            for side in range(2):
                for low in range(2):
                    both = jnp.stack([part[:, low, side] for part in parts], axis=1)
                    dcat[side, half, pl.ds(low * 128, 128), lanes] = both.reshape(128, 128).astype(BF16)
            return 0

        lax.fori_loop(0, 8, per_block, 0)

    def arrange(parity, half):
        for side in range(2):
            for part in range(2):
                moved = lax.dot_general(
                    one[pl.ds(parity * 512 + part * 256, 256), :],
                    dcat[side, half],
                    NT,
                    preferred_element_type=F32,
                ).astype(BF16)
                for low in range(2):
                    send1[parity, half, side, low, pl.ds(part * 256, 256), :] = moved[:, low * 128 : (low + 1) * 128]
        x_ref[parity, half, :, :, mine, :] = send1[parity, half, :, :, mine, :]

    def spread_dressed(*where):
        spread(send1.at[where], x_ref.at[where], send1_sem.at[where], recv1_sem.at[where])

    def await_dressed(*where):
        await_peers(x_ref.at[where], recv1_sem.at[where])

    def shifts(chunk, half):
        piece = pl.ds(half * 8, 8)
        return [
            pltpu.make_async_remote_copy(
                src_ref=strips[chunk].at[piece],
                dst_ref=target[chunk].at[piece],
                send_sem=shift_send_sem.at[way, chunk, half],
                recv_sem=shift_recv_sem.at[way, chunk, half],
                device_id=(other, me),
                device_id_type=MESH,
            )
            for way, (target, other) in enumerate(((low_ref, above), (high_ref, below)))
        ]

    def start_shifts(chunk, half):
        for copy in shifts(chunk, half):
            copy.start()

    def make_strips(parity, half, sides):
        rows = jnp.concatenate([x_ref[parity, half, side].reshape(1024, 128).T for side in sides], axis=0)
        moved = jnp.dot(rows, two[...], preferred_element_type=F32).astype(BF16)
        for at, side in enumerate(sides):
            for place in range(8):
                for k in range(8):
                    strips[2 * parity + side][half * 8 + place, :, pl.ds(k * 128, 128)] = moved[
                        at * 128 + k * 16 : at * 128 + (k + 1) * 16, place * 128 : (place + 1) * 128
                    ]

    def make_scale(chunk):
        parity, side = chunk // 2, chunk % 2

        def per_block(n, _):
            row = lax.broadcasted_iota(jnp.int32, (8, 128), 0)
            lane = lax.broadcasted_iota(jnp.int32, (8, 128), 1)
            own = vir[n, 2 * me + parity]
            per_row = jnp.zeros((8, 128), F32)
            for j in range(8):
                per_row = jnp.where(row == j, own - occ[n, side * 8 + j], per_row)
            both = vir_rows[pl.ds(n, 1), :]
            both = jnp.broadcast_to(jnp.concatenate((both, both), axis=1), (8, 128))
            for pair in range(8):
                per_lane = both - jnp.where(lane < 64, occ[n, 2 * pair], occ[n, 2 * pair + 1])
                scale[n, :, pl.ds(pair * 128, 128)] = 1.0 / (per_row + per_lane)
            return 0

        lax.fori_loop(0, 16, per_block, 0)

    def pick(chunk, q, source):
        def per_block(n, _):
            picked[q, pl.ds(pl.multiple_of(n * 16, 16), 16), :] = source[chunk][partner[q, n]]
            return 0

        lax.fori_loop(0, 16, per_block, 0)

    def own_cycle(chunk):
        pick(chunk, 0, strips)

        def columns(step, _):
            span = pl.ds(pl.multiple_of(step * 256, 256), 256)
            for part in range(2):
                total[part, :, span] = jnp.dot(picked[0], w_ref[0, part, :, span], preferred_element_type=F32)
            return 0

        lax.fori_loop(0, 4, columns, 0)
        make_scale(chunk)

    def far_cycle(chunk):
        for half in range(2):
            for copy in shifts(chunk, half):
                copy.wait_recv()
        pick(chunk, 1, low_ref)
        pick(chunk, 2, high_ref)
        parity, side = chunk // 2, chunk % 2

        def columns(step, _):
            span = pl.ds(pl.multiple_of(step * 256, 256), 256)
            sums = []
            for part in range(2):
                some = total[part, :, span]
                for q in (1, 2):
                    some += jnp.dot(picked[q], w_ref[q, part, :, span], preferred_element_type=F32)
                sums.append(some.reshape(16, 2, 8, 256))
            by_real, by_imag = sums
            held = strips[chunk][:, :, span].astype(F32).reshape(16, 2, 8, 256)
            factor = scale[:, :, span]
            real = (held[:, 0] + (by_real[:, 0] - by_imag[:, 1])) * factor
            imag = (held[:, 1] + (by_imag[:, 0] + by_real[:, 1])) * factor
            result = jnp.stack((real, imag), axis=1).reshape(256, 256).astype(BF16)
            for n in range(16):
                half, place = n // 8, n % 8
                for pair in range(2):
                    rows = pl.ds(pl.multiple_of(half * 128 + step * 32 + pair * 16, 16), 16)
                    regroup[rows, pl.ds(place * 128, 128)] = result[
                        n * 16 : (n + 1) * 16, pair * 128 : (pair + 1) * 128
                    ]
            return 0

        lax.fori_loop(0, 4, columns, 0)
        for part in range(4):
            moved = lax.dot_general(
                two[pl.ds(part * 256, 256), :], regroup[...], NT, preferred_element_type=F32
            ).astype(BF16)
            for half in range(2):
                send2[parity, side, half, part // 2, pl.ds((part % 2) * 256, 256), :] = moved[
                    :, half * 128 : (half + 1) * 128
                ]
        y_ref[parity, side, :, :, mine, :] = send2[parity, side, :, :, mine, :]
        spread(send2.at[parity, side], y_ref.at[parity, side], send2_sem.at[parity, side], recv2_sem.at[parity, side])

    def unpacked(chunk, half):
        parity, side = chunk // 2, chunk % 2
        rows = jnp.concatenate([y_ref[parity, side, half, low].T for low in range(2)], axis=0)
        moved = jnp.dot(rows, one[pl.ds(parity * 512, 512), :], preferred_element_type=F32)
        return moved.reshape(2, 8, 2, 8, 1024)

    def store(half):
        span = pl.ds(half * 8, 8)
        return pltpu.make_async_copy(out.at[span], out_hbm.at[span], load_sem.at[5 + half])

    def finish(chunks):
        for chunk in chunks:
            where = chunk // 2, chunk % 2
            await_peers(y_ref.at[where], recv2_sem.at[where])
        for half in range(2):
            known = {chunk % 2: unpacked(chunk, half) for chunk in chunks}
            for place in range(8):
                for low in range(2):
                    for i in range(8):
                        for p in range(2):
                            tiles = [
                                known[side][low, i, p, :, place * 128 : (place + 1) * 128]
                                if side in known
                                else jnp.zeros((8, 128), F32)
                                for side in range(2)
                            ]
                            tile = jnp.concatenate(tiles, axis=0).astype(BF16)
                            spot = (half * 8 + place, p, pl.ds((i * 2 + low) * 16, 16))
                            out[spot] = tile if chunks[0] < 2 else out[spot] + tile
            if 3 in chunks:
                store(half).start()

    permutation(one, True)
    for copy in loads[0]:
        copy.wait()
    dress(0)
    arrange(0, 0)
    pl.semaphore_wait(barrier, RANKS + 1)
    spread_dressed(0, 0, 0)
    spread_dressed(0, 0, 1)
    for copy in loads[1]:
        copy.wait()
    dress(1)
    arrange(0, 1)
    permutation(two, False)
    await_dressed(0, 0, 0)
    make_strips(0, 0, (0,))
    start_shifts(0, 0)
    await_dressed(0, 0, 1)
    spread_dressed(0, 1, 0)
    spread_dressed(0, 1, 1)
    make_strips(0, 0, (1,))
    start_shifts(1, 0)
    arrange(1, 0)
    arrange(1, 1)

    def strips_both(parity, half):
        for side in range(2):
            await_dressed(parity, half, side)
        if (parity, half) != (1, 1):
            spread_dressed(1, parity, 0)
            spread_dressed(1, parity, 1)
        make_strips(parity, half, (0, 1))

    strips_both(0, 1)
    start_shifts(0, 1)
    start_shifts(1, 1)
    w_load.wait()
    own_cycle(0)
    strips_both(1, 0)
    start_shifts(2, 0)
    far_cycle(0)
    strips_both(1, 1)
    start_shifts(2, 1)
    start_shifts(3, 0)
    start_shifts(3, 1)
    own_cycle(1)
    far_cycle(1)
    own_cycle(2)
    far_cycle(2)
    own_cycle(3)
    finish((0, 1))
    far_cycle(3)
    finish((2,))
    finish((3,))
    for first in range(2):
        for second in range(2):
            for third in range(2):
                await_peers(send1.at[first, second, third], send1_sem.at[first, second, third])
            await_peers(send2.at[first, second], send2_sem.at[first, second])
    for chunk in range(4):
        for half in range(2):
            for copy in shifts(chunk, half):
                copy.wait_send()
    for half in range(2):
        store(half).wait()


def per_device(amplitudes, ladder, cycle, partner, occ_energy, vir_energy):
    hbm = pl.BlockSpec(memory_space=pltpu.HBM)
    smem = pl.BlockSpec(memory_space=pltpu.SMEM)
    vmem = pl.BlockSpec(memory_space=pltpu.VMEM)
    exchanged = pltpu.VMEM((2, 2, 2, 2, 512, 128), BF16)
    field = pltpu.VMEM((16, 16, 1024), BF16)
    square = pltpu.VMEM((1024, 1024), BF16)
    dma = pltpu.SemaphoreType.DMA
    return pl.pallas_call(
        kernel,
        out_shape=jax.ShapeDtypeStruct((16, 2, 256, 128), BF16),
        in_specs=[hbm, hbm, hbm, smem, smem, smem, vmem],
        out_specs=pl.BlockSpec(memory_space=pl.ANY),
        scratch_shapes=[
            pltpu.VMEM((16, 2, 256, 128), BF16),
            pltpu.VMEM((16, 2, 256, 256), BF16),
            pltpu.VMEM((3, 2, 1024, 1024), BF16),
            square,
            square,
            pltpu.VMEM((2, 2, 256, 1024), BF16),
            exchanged,
            exchanged,
            *[field] * 12,
            pltpu.VMEM((3, 256, 1024), BF16),
            pltpu.VMEM((2, 256, 1024), F32),
            pltpu.VMEM((16, 8, 1024), F32),
            pltpu.VMEM((256, 1024), BF16),
            pltpu.VMEM((16, 2, 256, 128), BF16),
            exchanged,
            exchanged,
            dma((7,)),
            dma((2, 2, 2)),
            dma((2, 2, 2)),
            dma((2, 4, 2)),
            dma((2, 4, 2)),
            dma((2, 2)),
            dma((2, 2)),
        ],
        compiler_params=pltpu.CompilerParams(
            collective_id=0, has_side_effects=True, vmem_limit_bytes=60 * 1024 * 1024
        ),
    )(amplitudes, ladder, cycle[0], partner.T, occ_energy, vir_energy, vir_energy)


def solution(mesh):
    return jax.shard_map(
        per_device,
        mesh=mesh,
        in_specs=(
            P("kgrp", None, None, "vpair"),
            P("kgrp", None, None, None),
            P("kgrp", None, None, None, None),
            P("kgrp", None),
            P("kgrp", None),
            P("kgrp", None),
        ),
        out_specs=P("kgrp", None, None, "vpair"),
        check_vma=False,
    )
```

```python
import jax
import jax.numpy as jnp
from jax import lax
from jax.experimental import pallas as pl
from jax.experimental.pallas import tpu as pltpu
from jax.sharding import PartitionSpec as P

F32 = jnp.float32
BF16 = jnp.bfloat16
NT = (((1,), (1,)), ((), ()))
MESH = pl.DeviceIdType.MESH
RANKS = 32
STRIDE = 1


def permutation(ref, swapped):
    def block(step, _):
        row = lax.broadcasted_iota(jnp.int32, (64, 1024), 0) + step * 64
        col = lax.broadcasted_iota(jnp.int32, (64, 1024), 1)
        x, r, n, y = row >> 9, (row >> 4) & 31, (row >> 1) & 7, row & 1
        if swapped:
            x, y = y, x
        target = n * 128 + x * 64 + r * 2 + y
        ref[pl.ds(pl.multiple_of(step * 64, 64), 64), :] = jnp.where(col == target, 1.0, 0.0).astype(BF16)
        return 0

    lax.fori_loop(0, 16, block, 0)


def kernel(
    t_hbm,
    l_hbm,
    w_hbm,
    partner_hbm,
    occ_hbm,
    vir_hbm,
    out_hbm,
    t_ref,
    l_ref,
    w_ref,
    one,
    two,
    dcat,
    send1,
    x_ref,
    *rest,
):
    strips, low_ref, high_ref = rest[:4], rest[4:8], rest[8:12]
    (
        picked,
        total,
        scale,
        regroup,
        out,
        partner,
        occ,
        vir,
        vir_rows,
        send2,
        y_ref,
        load_sem,
        send1_sem,
        recv1_sem,
        shift_send_sem,
        shift_recv_sem,
        send2_sem,
        recv2_sem,
    ) = rest[12:]
    group = lax.axis_index("kgrp")
    me = lax.axis_index("vpair")
    above, below = lax.rem(group + 1, 4), lax.rem(group + 3, 4)

    barrier = pltpu.get_barrier_semaphore()
    mine_x, mine_y, mine_core = me // 8, (me // 2) % 4, me % 2

    def peer_of(i):
        turn = lax.rem(i * STRIDE, RANKS)
        x = lax.rem(mine_x + turn // 8, 4)
        y = lax.rem(mine_y + lax.rem(turn // 2, 4), 4)
        return x * 8 + y * 2 + lax.rem(mine_core + turn, 2)

    def greet(i, _):
        pl.semaphore_signal(barrier, inc=1, device_id=(group, peer_of(i)), device_id_type=MESH)
        return 0

    lax.fori_loop(1, RANKS, greet, 0)
    for other in (above, below):
        pl.semaphore_signal(barrier, inc=1, device_id=(other, me), device_id_type=MESH)

    loads = []
    for half in range(2):
        span = pl.ds(half * 8, 8)
        loads.append(
            (
                pltpu.make_async_copy(t_hbm.at[span], t_ref.at[span], load_sem.at[2 * half]),
                pltpu.make_async_copy(l_hbm.at[span], l_ref.at[span], load_sem.at[2 * half + 1]),
            )
        )
    small = [
        pltpu.make_async_copy(source, target, load_sem.at[7 + at])
        for at, (source, target) in enumerate(
            ((partner_hbm, partner), (occ_hbm, occ), (vir_hbm, vir), (vir_hbm, vir_rows))
        )
    ]
    w_load = pltpu.make_async_copy(w_hbm, w_ref, load_sem.at[4])
    for pair in loads:
        for copy in pair:
            copy.start()
    for copy in small:
        copy.start()
    w_load.start()

    mine = pl.ds(pl.multiple_of(me * 16, 16), 16)

    def spread(source, target, send_sem, recv_sem):
        ahead = (slice(None),) * (len(source.shape) - 2)

        def one_peer(i, _):
            peer = peer_of(i)
            pltpu.make_async_remote_copy(
                src_ref=source.at[(*ahead, pl.ds(pl.multiple_of(peer * 16, 16), 16), slice(None))],
                dst_ref=target.at[(*ahead, mine, slice(None))],
                send_sem=send_sem,
                recv_sem=recv_sem,
                device_id=(group, peer),
                device_id_type=MESH,
            ).start()
            return 0

        lax.fori_loop(1, RANKS, one_peer, 0)

    def await_peers(ref, sem):
        ahead = (slice(None),) * (len(ref.shape) - 2)
        part = ref.at[(*ahead, pl.ds(0, 16 * (RANKS - 1)), slice(None))]
        pltpu.make_async_copy(part, part, sem).wait()

    def dress(half):
        def per_block(place, _):
            n = half * 8 + place
            weights = jnp.concatenate((t_ref[n, 0], t_ref[n, 1]), axis=1)
            real = jnp.dot(l_ref[n, 0], weights, preferred_element_type=F32)
            imag = jnp.dot(l_ref[n, 1], weights, preferred_element_type=F32)
            lanes = pl.ds(pl.multiple_of(place * 128, 128), 128)
            parts = (real[:, :128] - imag[:, 128:], real[:, 128:] + imag[:, :128])
            parts = [part.reshape(8, 2, 2, 8, 128) for part in parts]
            for side in range(2):
                for low in range(2):
                    both = jnp.stack([part[:, low, side] for part in parts], axis=1)
                    dcat[side, half, pl.ds(low * 128, 128), lanes] = both.reshape(128, 128).astype(BF16)
            return 0

        lax.fori_loop(0, 8, per_block, 0)

    def arrange(parity, half):
        for side in range(2):
            for part in range(2):
                moved = lax.dot_general(
                    one[pl.ds(parity * 512 + part * 256, 256), :],
                    dcat[side, half],
                    NT,
                    preferred_element_type=F32,
                ).astype(BF16)
                for low in range(2):
                    send1[parity, half, side, low, pl.ds(part * 256, 256), :] = moved[:, low * 128 : (low + 1) * 128]
        x_ref[parity, half, :, :, mine, :] = send1[parity, half, :, :, mine, :]

    def spread_dressed(*where):
        spread(send1.at[where], x_ref.at[where], send1_sem.at[where], recv1_sem.at[where])

    def await_dressed(*where):
        await_peers(x_ref.at[where], recv1_sem.at[where])

    def shifts(chunk, half):
        piece = pl.ds(half * 8, 8)
        return [
            pltpu.make_async_remote_copy(
                src_ref=strips[chunk].at[piece],
                dst_ref=target[chunk].at[piece],
                send_sem=shift_send_sem.at[way, chunk, half],
                recv_sem=shift_recv_sem.at[way, chunk, half],
                device_id=(other, me),
                device_id_type=MESH,
            )
            for way, (target, other) in enumerate(((low_ref, above), (high_ref, below)))
        ]

    def start_shifts(chunk, half):
        for copy in shifts(chunk, half):
            copy.start()

    def make_strips(parity, half, sides):
        rows = jnp.concatenate([x_ref[parity, half, side].reshape(1024, 128).T for side in sides], axis=0)
        moved = jnp.dot(rows, two[...], preferred_element_type=F32).astype(BF16)
        for at, side in enumerate(sides):
            for place in range(8):
                for k in range(8):
                    strips[2 * parity + side][half * 8 + place, :, pl.ds(k * 128, 128)] = moved[
                        at * 128 + k * 16 : at * 128 + (k + 1) * 16, place * 128 : (place + 1) * 128
                    ]

    def make_scale(chunk):
        parity, side = chunk // 2, chunk % 2

        def per_block(n, _):
            row = lax.broadcasted_iota(jnp.int32, (8, 128), 0)
            lane = lax.broadcasted_iota(jnp.int32, (8, 128), 1)
            own = vir[n, 2 * me + parity]
            per_row = jnp.zeros((8, 128), F32)
            for j in range(8):
                per_row = jnp.where(row == j, own - occ[n, side * 8 + j], per_row)
            both = vir_rows[pl.ds(n, 1), :]
            both = jnp.broadcast_to(jnp.concatenate((both, both), axis=1), (8, 128))
            for pair in range(8):
                per_lane = both - jnp.where(lane < 64, occ[n, 2 * pair], occ[n, 2 * pair + 1])
                scale[n, :, pl.ds(pair * 128, 128)] = 1.0 / (per_row + per_lane)
            return 0

        lax.fori_loop(0, 16, per_block, 0)

    def pick(chunk, q, source):
        def per_block(n, _):
            picked[q, pl.ds(pl.multiple_of(n * 16, 16), 16), :] = source[chunk][partner[q, n]]
            return 0

        lax.fori_loop(0, 16, per_block, 0)

    def own_cycle(chunk):
        pick(chunk, 0, strips)

        def columns(step, _):
            span = pl.ds(pl.multiple_of(step * 512, 512), 512)
            for part in range(2):
                total[part, :, span] = jnp.dot(picked[0], w_ref[0, part, :, span], preferred_element_type=F32)
            return 0

        lax.fori_loop(0, 2, columns, 0)
        make_scale(chunk)

    def far_cycle(chunk):
        for half in range(2):
            for copy in shifts(chunk, half):
                copy.wait_recv()
        pick(chunk, 1, low_ref)
        pick(chunk, 2, high_ref)
        parity, side = chunk // 2, chunk % 2
        for step in range(2):
            span = pl.ds(step * 512, 512)
            sums = []
            for part in range(2):
                some = total[part, :, span]
                for q in (1, 2):
                    some += jnp.dot(picked[q], w_ref[q, part, :, span], preferred_element_type=F32)
                sums.append(some.reshape(16, 2, 8, 512))
            by_real, by_imag = sums
            held = strips[chunk][:, :, span].astype(F32).reshape(16, 2, 8, 512)
            factor = scale[:, :, span]
            real = (held[:, 0] + (by_real[:, 0] - by_imag[:, 1])) * factor
            imag = (held[:, 1] + (by_imag[:, 0] + by_real[:, 1])) * factor
            result = jnp.stack((real, imag), axis=1).reshape(256, 512).astype(BF16)
            for n in range(16):
                half, place = n // 8, n % 8
                for pair in range(4):
                    regroup[pl.ds(half * 64 + pair * 16, 16), pl.ds(place * 128, 128)] = result[
                        n * 16 : (n + 1) * 16, pair * 128 : (pair + 1) * 128
                    ]
            for part in range(4):
                send2[parity, side, step, part // 2, pl.ds((part % 2) * 256, 256), :] = lax.dot_general(
                    two[pl.ds(part * 256, 256), :], regroup[...], NT, preferred_element_type=F32
                ).astype(BF16)
            where = parity, side, step
            y_ref[(*where, slice(None), mine)] = send2[(*where, slice(None), mine)]
            spread(send2.at[where], y_ref.at[where], send2_sem.at[where], recv2_sem.at[where])

    def store(step):
        span = pl.ds(step * 128, 128)
        return pltpu.make_async_copy(out.at[:, :, span], out_hbm.at[:, :, span], load_sem.at[5 + step])

    def unpacked(chunk, step):
        where = chunk // 2, chunk % 2, step
        await_peers(y_ref.at[where], recv2_sem.at[where])
        rows = jnp.concatenate([y_ref[(*where, low)].T for low in range(2)], axis=0)
        moved = jnp.dot(rows, one[pl.ds(where[0] * 512, 512), :], preferred_element_type=F32)
        return moved.reshape(2, 2, 4, 2, 8, 1024)

    def finish(chunks):
        for step in range(2):
            known = {chunk % 2: unpacked(chunk, step) for chunk in chunks}
            for place in range(8):
                for low in range(2):
                    for half in range(2):
                        for i in range(4):
                            for p in range(2):
                                tiles = [
                                    known[side][low, half, i, p, :, place * 128 : (place + 1) * 128]
                                    if side in known
                                    else jnp.zeros((8, 128), F32)
                                    for side in range(2)
                                ]
                                tile = jnp.concatenate(tiles, axis=0).astype(BF16)
                                spot = (half * 8 + place, p, pl.ds(((step * 4 + i) * 2 + low) * 16, 16))
                                out[spot] = tile if chunks[0] < 2 else out[spot] + tile
            if 3 in chunks:
                store(step).start()

    permutation(one, True)
    for copy in loads[0]:
        copy.wait()
    dress(0)
    arrange(0, 0)
    pl.semaphore_wait(barrier, RANKS + 1)
    spread_dressed(0, 0, 0)
    spread_dressed(0, 0, 1)
    for copy in loads[1]:
        copy.wait()
    dress(1)
    arrange(0, 1)
    permutation(two, False)
    await_dressed(0, 0, 0)
    make_strips(0, 0, (0,))
    start_shifts(0, 0)
    await_dressed(0, 0, 1)
    spread_dressed(0, 1, 0)
    spread_dressed(0, 1, 1)
    make_strips(0, 0, (1,))
    start_shifts(1, 0)
    arrange(1, 0)
    arrange(1, 1)

    def strips_both(parity, half):
        for side in range(2):
            await_dressed(parity, half, side)
        if (parity, half) != (1, 1):
            spread_dressed(1, parity, 0)
            spread_dressed(1, parity, 1)
        make_strips(parity, half, (0, 1))

    strips_both(0, 1)
    start_shifts(0, 1)
    start_shifts(1, 1)
    w_load.wait()
    for copy in small:
        copy.wait()
    own_cycle(0)
    strips_both(1, 0)
    start_shifts(2, 0)
    far_cycle(0)
    strips_both(1, 1)
    start_shifts(2, 1)
    start_shifts(3, 0)
    start_shifts(3, 1)
    own_cycle(1)
    far_cycle(1)
    own_cycle(2)
    far_cycle(2)
    own_cycle(3)
    far_cycle(3)
    finish((0, 1))
    finish((2,))
    finish((3,))
    for first in range(2):
        for second in range(2):
            for third in range(2):
                await_peers(send1.at[first, second, third], send1_sem.at[first, second, third])
                await_peers(send2.at[first, second, third], send2_sem.at[first, second, third])
    for chunk in range(4):
        for half in range(2):
            for copy in shifts(chunk, half):
                copy.wait_send()
    for half in range(2):
        store(half).wait()


def per_device(amplitudes, ladder, cycle, partner, occ_energy, vir_energy):
    hbm = pl.BlockSpec(memory_space=pltpu.HBM)
    exchanged = pltpu.VMEM((2, 2, 2, 2, 512, 128), BF16)
    field = pltpu.VMEM((16, 16, 1024), BF16)
    square = pltpu.VMEM((1024, 1024), BF16)
    dma = pltpu.SemaphoreType.DMA
    return pl.pallas_call(
        kernel,
        out_shape=jax.ShapeDtypeStruct((16, 2, 256, 128), BF16),
        in_specs=[hbm] * 6,
        out_specs=pl.BlockSpec(memory_space=pl.ANY),
        scratch_shapes=[
            pltpu.VMEM((16, 2, 256, 128), BF16),
            pltpu.VMEM((16, 2, 256, 256), BF16),
            pltpu.VMEM((3, 2, 1024, 1024), BF16),
            square,
            square,
            pltpu.VMEM((2, 2, 256, 1024), BF16),
            exchanged,
            exchanged,
            *[field] * 12,
            pltpu.VMEM((3, 256, 1024), BF16),
            pltpu.VMEM((2, 256, 1024), F32),
            pltpu.VMEM((16, 8, 1024), F32),
            pltpu.VMEM((128, 1024), BF16),
            pltpu.VMEM((16, 2, 256, 128), BF16),
            pltpu.SMEM((3, 16), jnp.int32),
            pltpu.SMEM((16, 16), F32),
            pltpu.SMEM((16, 64), F32),
            pltpu.VMEM((16, 64), F32),
            exchanged,
            exchanged,
            dma((11,)),
            dma((2, 2, 2)),
            dma((2, 2, 2)),
            dma((2, 4, 2)),
            dma((2, 4, 2)),
            dma((2, 2, 2)),
            dma((2, 2, 2)),
        ],
        compiler_params=pltpu.CompilerParams(
            collective_id=0, has_side_effects=True, vmem_limit_bytes=60 * 1024 * 1024
        ),
    )(amplitudes, ladder, cycle[0], partner.T, occ_energy, vir_energy)


def solution(mesh):
    return jax.shard_map(
        per_device,
        mesh=mesh,
        in_specs=(
            P("kgrp", None, None, "vpair"),
            P("kgrp", None, None, None),
            P("kgrp", None, None, None, None),
            P("kgrp", None),
            P("kgrp", None),
            P("kgrp", None),
        ),
        out_specs=P("kgrp", None, None, "vpair"),
        check_vma=False,
    )
```

```python
import jax
import jax.numpy as jnp
from jax import lax
from jax.experimental import pallas as pl
from jax.experimental.pallas import tpu as pltpu
from jax.sharding import PartitionSpec as P

F32 = jnp.float32
BF16 = jnp.bfloat16
NT = (((1,), (1,)), ((), ()))
MESH = pl.DeviceIdType.MESH
RANKS = 32
STRIDE = 1


def permutation(ref, swapped):
    def block(step, _):
        row = lax.broadcasted_iota(jnp.int32, (64, 1024), 0) + step * 64
        col = lax.broadcasted_iota(jnp.int32, (64, 1024), 1)
        x, r, n, y = row >> 9, (row >> 4) & 31, (row >> 1) & 7, row & 1
        if swapped:
            x, y = y, x
        target = n * 128 + x * 64 + r * 2 + y
        ref[pl.ds(pl.multiple_of(step * 64, 64), 64), :] = jnp.where(col == target, 1.0, 0.0).astype(BF16)
        return 0

    lax.fori_loop(0, 16, block, 0)


def kernel(
    t_hbm,
    l_hbm,
    w_hbm,
    partner_hbm,
    occ_hbm,
    vir_hbm,
    out_hbm,
    t_ref,
    l_ref,
    w_ref,
    one,
    two,
    dcat,
    send1,
    x_ref,
    *rest,
):
    strips, low_ref, high_ref = rest[:4], rest[4:8], rest[8:12]
    (
        picked,
        total,
        scale,
        regroup,
        out,
        partner,
        occ,
        vir,
        vir_rows,
        send2,
        y_ref,
        load_sem,
        send1_sem,
        recv1_sem,
        shift_send_sem,
        shift_recv_sem,
        send2_sem,
        recv2_sem,
    ) = rest[12:]
    group = lax.axis_index("kgrp")
    me = lax.axis_index("vpair")
    above, below = lax.rem(group + 1, 4), lax.rem(group + 3, 4)

    barrier = pltpu.get_barrier_semaphore()
    mine_x, mine_y, mine_core = me // 8, (me // 2) % 4, me % 2

    def peer_of(i):
        turn = lax.rem(i * STRIDE, RANKS)
        x = lax.rem(mine_x + turn // 8, 4)
        y = lax.rem(mine_y + lax.rem(turn // 2, 4), 4)
        return x * 8 + y * 2 + lax.rem(mine_core + turn, 2)

    def greet(i, _):
        pl.semaphore_signal(barrier, inc=1, device_id=(group, peer_of(i)), device_id_type=MESH)
        return 0

    lax.fori_loop(1, RANKS, greet, 0)
    for other in (above, below):
        pl.semaphore_signal(barrier, inc=1, device_id=(other, me), device_id_type=MESH)

    loads = []
    for half in range(2):
        span = pl.ds(half * 8, 8)
        loads.append(
            (
                pltpu.make_async_copy(t_hbm.at[span], t_ref.at[span], load_sem.at[2 * half]),
                pltpu.make_async_copy(l_hbm.at[span], l_ref.at[span], load_sem.at[2 * half + 1]),
            )
        )
    small = [
        pltpu.make_async_copy(source, target, load_sem.at[7 + at])
        for at, (source, target) in enumerate(
            ((partner_hbm, partner), (occ_hbm, occ), (vir_hbm, vir), (vir_hbm, vir_rows))
        )
    ]
    w_load = pltpu.make_async_copy(w_hbm, w_ref, load_sem.at[4])
    for pair in loads:
        for copy in pair:
            copy.start()
    for copy in small:
        copy.start()
    w_load.start()

    mine = pl.ds(pl.multiple_of(me * 16, 16), 16)

    def spread(source, target, send_sem, recv_sem):
        ahead = (slice(None),) * (len(source.shape) - 2)

        def one_peer(i, _):
            peer = peer_of(i)
            pltpu.make_async_remote_copy(
                src_ref=source.at[(*ahead, pl.ds(pl.multiple_of(peer * 16, 16), 16), slice(None))],
                dst_ref=target.at[(*ahead, mine, slice(None))],
                send_sem=send_sem,
                recv_sem=recv_sem,
                device_id=(group, peer),
                device_id_type=MESH,
            ).start()
            return 0

        lax.fori_loop(1, RANKS, one_peer, 0)

    def await_peers(ref, sem):
        ahead = (slice(None),) * (len(ref.shape) - 2)
        part = ref.at[(*ahead, pl.ds(0, 16 * (RANKS - 1)), slice(None))]
        pltpu.make_async_copy(part, part, sem).wait()

    def dress(half):
        def per_block(place, _):
            n = half * 8 + place
            weights = jnp.concatenate((t_ref[n, 0], t_ref[n, 1]), axis=1)
            real = jnp.dot(l_ref[n, 0], weights, preferred_element_type=F32)
            imag = jnp.dot(l_ref[n, 1], weights, preferred_element_type=F32)
            lanes = pl.ds(pl.multiple_of(place * 128, 128), 128)
            parts = (real[:, :128] - imag[:, 128:], real[:, 128:] + imag[:, :128])
            parts = [part.reshape(8, 2, 2, 8, 128) for part in parts]
            for side in range(2):
                for low in range(2):
                    both = jnp.stack([part[:, low, side] for part in parts], axis=1)
                    dcat[side, half, pl.ds(low * 128, 128), lanes] = both.reshape(128, 128).astype(BF16)
            return 0

        lax.fori_loop(0, 8, per_block, 0)

    def arrange(parity, half):
        for side in range(2):
            for part in range(2):
                moved = lax.dot_general(
                    one[pl.ds(parity * 512 + part * 256, 256), :],
                    dcat[side, half],
                    NT,
                    preferred_element_type=F32,
                ).astype(BF16)
                for low in range(2):
                    send1[parity, half, side, low, pl.ds(part * 256, 256), :] = moved[:, low * 128 : (low + 1) * 128]
        x_ref[parity, half, :, :, mine, :] = send1[parity, half, :, :, mine, :]

    def spread_dressed(*where):
        spread(send1.at[where], x_ref.at[where], send1_sem.at[where], recv1_sem.at[where])

    def await_dressed(*where):
        await_peers(x_ref.at[where], recv1_sem.at[where])

    def shifts(chunk, half):
        piece = pl.ds(half * 8, 8)
        return [
            pltpu.make_async_remote_copy(
                src_ref=strips[chunk].at[piece],
                dst_ref=target[chunk].at[piece],
                send_sem=shift_send_sem.at[way, chunk, half],
                recv_sem=shift_recv_sem.at[way, chunk, half],
                device_id=(other, me),
                device_id_type=MESH,
            )
            for way, (target, other) in enumerate(((low_ref, above), (high_ref, below)))
        ]

    def start_shifts(chunk, half):
        for copy in shifts(chunk, half):
            copy.start()

    def make_strips(parity, half, sides):
        rows = jnp.concatenate([x_ref[parity, half, side].reshape(1024, 128).T for side in sides], axis=0)
        moved = jnp.dot(rows, two[...], preferred_element_type=F32).astype(BF16)
        for at, side in enumerate(sides):
            for place in range(8):
                for k in range(8):
                    strips[2 * parity + side][half * 8 + place, :, pl.ds(k * 128, 128)] = moved[
                        at * 128 + k * 16 : at * 128 + (k + 1) * 16, place * 128 : (place + 1) * 128
                    ]

    def make_scale(chunk):
        parity, side = chunk // 2, chunk % 2

        def per_block(n, _):
            row = lax.broadcasted_iota(jnp.int32, (8, 128), 0)
            lane = lax.broadcasted_iota(jnp.int32, (8, 128), 1)
            own = vir[n, 2 * me + parity]
            per_row = jnp.zeros((8, 128), F32)
            for j in range(8):
                per_row = jnp.where(row == j, own - occ[n, side * 8 + j], per_row)
            both = vir_rows[pl.ds(n, 1), :]
            both = jnp.broadcast_to(jnp.concatenate((both, both), axis=1), (8, 128))
            for pair in range(8):
                per_lane = both - jnp.where(lane < 64, occ[n, 2 * pair], occ[n, 2 * pair + 1])
                scale[side, n, :, pl.ds(pair * 128, 128)] = 1.0 / (per_row + per_lane)
            return 0

        lax.fori_loop(0, 16, per_block, 0)

    def pick(chunk, q, source):
        def per_block(n, _):
            picked[q, pl.ds(pl.multiple_of(n * 16, 16), 16), :] = source[chunk][partner[q, n]]
            return 0

        lax.fori_loop(0, 16, per_block, 0)

    def own_cycle(chunk):
        pick(chunk, 0, strips)

        def columns(step, _):
            span = pl.ds(pl.multiple_of(step * 512, 512), 512)
            for part in range(2):
                total[chunk % 2, part, :, span] = jnp.dot(picked[0], w_ref[0, part, :, span], preferred_element_type=F32)
            return 0

        lax.fori_loop(0, 2, columns, 0)
        make_scale(chunk)

    def far_cycle(chunk):
        for half in range(2):
            for copy in shifts(chunk, half):
                copy.wait_recv()
        pick(chunk, 1, low_ref)
        pick(chunk, 2, high_ref)
        parity, side = chunk // 2, chunk % 2
        for step in range(2):
            span = pl.ds(step * 512, 512)
            sums = []
            for part in range(2):
                some = total[side, part, :, span]
                for q in (1, 2):
                    some += jnp.dot(picked[q], w_ref[q, part, :, span], preferred_element_type=F32)
                sums.append(some.reshape(16, 2, 8, 512))
            by_real, by_imag = sums
            held = strips[chunk][:, :, span].astype(F32).reshape(16, 2, 8, 512)
            factor = scale[side, :, :, span]
            real = (held[:, 0] + (by_real[:, 0] - by_imag[:, 1])) * factor
            imag = (held[:, 1] + (by_imag[:, 0] + by_real[:, 1])) * factor
            result = jnp.stack((real, imag), axis=1).reshape(256, 512).astype(BF16)
            for n in range(16):
                half, place = n // 8, n % 8
                for pair in range(4):
                    regroup[pl.ds(half * 64 + pair * 16, 16), pl.ds(place * 128, 128)] = result[
                        n * 16 : (n + 1) * 16, pair * 128 : (pair + 1) * 128
                    ]
            for part in range(4):
                send2[parity, side, step, part // 2, pl.ds((part % 2) * 256, 256), :] = lax.dot_general(
                    two[pl.ds(part * 256, 256), :], regroup[...], NT, preferred_element_type=F32
                ).astype(BF16)
            where = parity, side, step
            y_ref[(*where, slice(None), mine)] = send2[(*where, slice(None), mine)]
            spread(send2.at[where], y_ref.at[where], send2_sem.at[where], recv2_sem.at[where])

    def store(step):
        span = pl.ds(step * 128, 128)
        return pltpu.make_async_copy(out.at[:, :, span], out_hbm.at[:, :, span], load_sem.at[5 + step])

    def unpacked(chunk, step):
        where = chunk // 2, chunk % 2, step
        await_peers(y_ref.at[where], recv2_sem.at[where])
        rows = jnp.concatenate([y_ref[(*where, low)].T for low in range(2)], axis=0)
        moved = jnp.dot(rows, one[pl.ds(where[0] * 512, 512), :], preferred_element_type=F32)
        return moved.reshape(2, 2, 4, 2, 8, 1024)

    def finish(chunks):
        for step in range(2):
            known = {chunk % 2: unpacked(chunk, step) for chunk in chunks}
            for place in range(8):
                for low in range(2):
                    for half in range(2):
                        for i in range(4):
                            for p in range(2):
                                tiles = [
                                    known[side][low, half, i, p, :, place * 128 : (place + 1) * 128]
                                    if side in known
                                    else jnp.zeros((8, 128), F32)
                                    for side in range(2)
                                ]
                                tile = jnp.concatenate(tiles, axis=0).astype(BF16)
                                spot = (half * 8 + place, p, pl.ds(((step * 4 + i) * 2 + low) * 16, 16))
                                out[spot] = tile if chunks[0] < 2 else out[spot] + tile
            if 3 in chunks:
                store(step).start()

    permutation(one, True)
    for copy in loads[0]:
        copy.wait()
    dress(0)
    arrange(0, 0)
    pl.semaphore_wait(barrier, RANKS + 1)
    spread_dressed(0, 0, 0)
    spread_dressed(0, 0, 1)
    for copy in loads[1]:
        copy.wait()
    dress(1)
    arrange(0, 1)
    permutation(two, False)
    await_dressed(0, 0, 0)
    make_strips(0, 0, (0,))
    start_shifts(0, 0)
    await_dressed(0, 0, 1)
    spread_dressed(0, 1, 0)
    spread_dressed(0, 1, 1)
    make_strips(0, 0, (1,))
    start_shifts(1, 0)
    arrange(1, 0)
    arrange(1, 1)

    def strips_both(parity, half):
        for side in range(2):
            await_dressed(parity, half, side)
        if (parity, half) != (1, 1):
            spread_dressed(1, parity, 0)
            spread_dressed(1, parity, 1)
        make_strips(parity, half, (0, 1))

    strips_both(0, 1)
    start_shifts(0, 1)
    start_shifts(1, 1)
    w_load.wait()
    for copy in small:
        copy.wait()
    own_cycle(0)
    own_cycle(1)
    strips_both(1, 0)
    start_shifts(2, 0)
    far_cycle(0)
    strips_both(1, 1)
    start_shifts(2, 1)
    start_shifts(3, 0)
    start_shifts(3, 1)
    far_cycle(1)
    own_cycle(2)
    own_cycle(3)
    far_cycle(2)
    finish((0, 1))
    far_cycle(3)
    finish((2,))
    finish((3,))
    for first in range(2):
        for second in range(2):
            for third in range(2):
                await_peers(send1.at[first, second, third], send1_sem.at[first, second, third])
                await_peers(send2.at[first, second, third], send2_sem.at[first, second, third])
    for chunk in range(4):
        for half in range(2):
            for copy in shifts(chunk, half):
                copy.wait_send()
    for half in range(2):
        store(half).wait()


def per_device(amplitudes, ladder, cycle, partner, occ_energy, vir_energy):
    hbm = pl.BlockSpec(memory_space=pltpu.HBM)
    exchanged = pltpu.VMEM((2, 2, 2, 2, 512, 128), BF16)
    field = pltpu.VMEM((16, 16, 1024), BF16)
    square = pltpu.VMEM((1024, 1024), BF16)
    dma = pltpu.SemaphoreType.DMA
    return pl.pallas_call(
        kernel,
        out_shape=jax.ShapeDtypeStruct((16, 2, 256, 128), BF16),
        in_specs=[hbm] * 6,
        out_specs=pl.BlockSpec(memory_space=pl.ANY),
        scratch_shapes=[
            pltpu.VMEM((16, 2, 256, 128), BF16),
            pltpu.VMEM((16, 2, 256, 256), BF16),
            pltpu.VMEM((3, 2, 1024, 1024), BF16),
            square,
            square,
            pltpu.VMEM((2, 2, 256, 1024), BF16),
            exchanged,
            exchanged,
            *[field] * 12,
            pltpu.VMEM((3, 256, 1024), BF16),
            pltpu.VMEM((2, 2, 256, 1024), F32),
            pltpu.VMEM((2, 16, 8, 1024), F32),
            pltpu.VMEM((128, 1024), BF16),
            pltpu.VMEM((16, 2, 256, 128), BF16),
            pltpu.SMEM((3, 16), jnp.int32),
            pltpu.SMEM((16, 16), F32),
            pltpu.SMEM((16, 64), F32),
            pltpu.VMEM((16, 64), F32),
            exchanged,
            exchanged,
            dma((11,)),
            dma((2, 2, 2)),
            dma((2, 2, 2)),
            dma((2, 4, 2)),
            dma((2, 4, 2)),
            dma((2, 2, 2)),
            dma((2, 2, 2)),
        ],
        compiler_params=pltpu.CompilerParams(
            collective_id=0, has_side_effects=True, vmem_limit_bytes=60 * 1024 * 1024
        ),
    )(amplitudes, ladder, cycle[0], partner.T, occ_energy, vir_energy)


def solution(mesh):
    return jax.shard_map(
        per_device,
        mesh=mesh,
        in_specs=(
            P("kgrp", None, None, "vpair"),
            P("kgrp", None, None, None),
            P("kgrp", None, None, None, None),
            P("kgrp", None),
            P("kgrp", None),
            P("kgrp", None),
        ),
        out_specs=P("kgrp", None, None, "vpair"),
        check_vma=False,
    )
```

```python
import jax
import jax.numpy as jnp
from jax import lax
from jax.experimental import pallas as pl
from jax.experimental.pallas import tpu as pltpu
from jax.sharding import PartitionSpec as P

F32 = jnp.float32
BF16 = jnp.bfloat16
NT = (((1,), (1,)), ((), ()))
MESH = pl.DeviceIdType.MESH
RANKS = 32
STRIDE = 1
CUT = 768


def permutation(ref, swapped):
    def block(step, _):
        row = lax.broadcasted_iota(jnp.int32, (64, 1024), 0) + step * 64
        col = lax.broadcasted_iota(jnp.int32, (64, 1024), 1)
        x, r, n, y = row >> 9, (row >> 4) & 31, (row >> 1) & 7, row & 1
        if swapped:
            x, y = y, x
        target = n * 128 + x * 64 + r * 2 + y
        ref[pl.ds(pl.multiple_of(step * 64, 64), 64), :] = jnp.where(col == target, 1.0, 0.0).astype(BF16)
        return 0

    lax.fori_loop(0, 16, block, 0)


def kernel(
    t_hbm,
    l_hbm,
    w_hbm,
    partner_hbm,
    occ_hbm,
    vir_hbm,
    out_hbm,
    t_ref,
    l_ref,
    w_ref,
    one,
    two,
    dcat,
    send1,
    x_ref,
    *rest,
):
    strips, low_ref, high_ref = rest[:4], (*rest[4:7], rest[7:9]), (*rest[9:12], rest[12:14])
    (
        picked,
        total,
        scale,
        regroup,
        out,
        partner,
        occ,
        vir,
        vir_rows,
        send2,
        y_ref,
        load_sem,
        send1_sem,
        recv1_sem,
        shift_send_sem,
        shift_recv_sem,
        send2_sem,
        recv2_sem,
    ) = rest[14:]
    group = lax.axis_index("kgrp")
    me = lax.axis_index("vpair")
    above, below = lax.rem(group + 1, 4), lax.rem(group + 3, 4)

    barrier = pltpu.get_barrier_semaphore()
    mine_x, mine_y, mine_core = me // 8, (me // 2) % 4, me % 2

    def peer_of(i):
        turn = lax.rem(i * STRIDE, RANKS)
        x = lax.rem(mine_x + turn // 8, 4)
        y = lax.rem(mine_y + lax.rem(turn // 2, 4), 4)
        return x * 8 + y * 2 + lax.rem(mine_core + turn, 2)

    def greet(i, _):
        pl.semaphore_signal(barrier, inc=1, device_id=(group, peer_of(i)), device_id_type=MESH)
        return 0

    lax.fori_loop(1, RANKS, greet, 0)
    for other in (above, below):
        pl.semaphore_signal(barrier, inc=1, device_id=(other, me), device_id_type=MESH)

    loads = []
    for half in range(2):
        span = pl.ds(half * 8, 8)
        loads.append(
            (
                pltpu.make_async_copy(t_hbm.at[span], t_ref.at[span], load_sem.at[2 * half]),
                pltpu.make_async_copy(l_hbm.at[span], l_ref.at[span], load_sem.at[2 * half + 1]),
            )
        )
    small = [
        pltpu.make_async_copy(source, target, load_sem.at[7 + at])
        for at, (source, target) in enumerate(
            ((partner_hbm, partner), (occ_hbm, occ), (vir_hbm, vir), (vir_hbm, vir_rows))
        )
    ]
    w_load = pltpu.make_async_copy(w_hbm, w_ref, load_sem.at[4])
    for pair in loads:
        for copy in pair:
            copy.start()
    for copy in small:
        copy.start()
    w_load.start()

    mine = pl.ds(pl.multiple_of(me * 16, 16), 16)

    def spread(source, target, send_sem, recv_sem):
        ahead = (slice(None),) * (len(source.shape) - 2)

        def one_peer(i, _):
            peer = peer_of(i)
            pltpu.make_async_remote_copy(
                src_ref=source.at[(*ahead, pl.ds(pl.multiple_of(peer * 16, 16), 16), slice(None))],
                dst_ref=target.at[(*ahead, mine, slice(None))],
                send_sem=send_sem,
                recv_sem=recv_sem,
                device_id=(group, peer),
                device_id_type=MESH,
            ).start()
            return 0

        lax.fori_loop(1, RANKS, one_peer, 0)

    def await_peers(ref, sem):
        ahead = (slice(None),) * (len(ref.shape) - 2)
        part = ref.at[(*ahead, pl.ds(0, 16 * (RANKS - 1)), slice(None))]
        pltpu.make_async_copy(part, part, sem).wait()

    def dress(half):
        def per_block(place, _):
            n = half * 8 + place
            weights = jnp.concatenate((t_ref[n, 0], t_ref[n, 1]), axis=1)
            real = jnp.dot(l_ref[n, 0], weights, preferred_element_type=F32)
            imag = jnp.dot(l_ref[n, 1], weights, preferred_element_type=F32)
            lanes = pl.ds(pl.multiple_of(place * 128, 128), 128)
            parts = (real[:, :128] - imag[:, 128:], real[:, 128:] + imag[:, :128])
            parts = [part.reshape(8, 2, 2, 8, 128) for part in parts]
            for side in range(2):
                for low in range(2):
                    both = jnp.stack([part[:, low, side] for part in parts], axis=1)
                    dcat[side, half, pl.ds(low * 128, 128), lanes] = both.reshape(128, 128).astype(BF16)
            return 0

        lax.fori_loop(0, 8, per_block, 0)

    def arrange(parity, half):
        for side in range(2):
            for part in range(2):
                moved = lax.dot_general(
                    one[pl.ds(parity * 512 + part * 256, 256), :],
                    dcat[side, half],
                    NT,
                    preferred_element_type=F32,
                ).astype(BF16)
                for low in range(2):
                    send1[parity, half, side, low, pl.ds(part * 256, 256), :] = moved[:, low * 128 : (low + 1) * 128]
        x_ref[parity, half, :, :, mine, :] = send1[parity, half, :, :, mine, :]

    def spread_dressed(*where):
        spread(send1.at[where], x_ref.at[where], send1_sem.at[where], recv1_sem.at[where])

    def await_dressed(*where):
        await_peers(x_ref.at[where], recv1_sem.at[where])

    def shifts(chunk, half):
        if chunk == 3:
            source = strips[3].at[:, :, pl.ds(CUT * half, CUT + half * (1024 - 2 * CUT))]
        else:
            source = strips[chunk].at[pl.ds(half * 8, 8)]
        return [
            pltpu.make_async_remote_copy(
                src_ref=source,
                dst_ref=target[3][half] if chunk == 3 else target[chunk].at[pl.ds(half * 8, 8)],
                send_sem=shift_send_sem.at[way, chunk, half],
                recv_sem=shift_recv_sem.at[way, chunk, half],
                device_id=(other, me),
                device_id_type=MESH,
            )
            for way, (target, other) in enumerate(((low_ref, above), (high_ref, below)))
        ]

    def start_shifts(chunk, half):
        for copy in shifts(chunk, half):
            copy.start()

    def make_strips(parity, half, sides):
        rows = jnp.concatenate([x_ref[parity, half, side].reshape(1024, 128).T for side in sides], axis=0)
        moved = jnp.dot(rows, two[...], preferred_element_type=F32).astype(BF16)
        for at, side in enumerate(sides):
            for place in range(8):
                for k in range(8):
                    strips[2 * parity + side][half * 8 + place, :, pl.ds(k * 128, 128)] = moved[
                        at * 128 + k * 16 : at * 128 + (k + 1) * 16, place * 128 : (place + 1) * 128
                    ]

    def make_scale(chunk):
        parity, side = chunk // 2, chunk % 2

        def per_block(n, _):
            row = lax.broadcasted_iota(jnp.int32, (8, 128), 0)
            lane = lax.broadcasted_iota(jnp.int32, (8, 128), 1)
            own = vir[n, 2 * me + parity]
            per_row = jnp.zeros((8, 128), F32)
            for j in range(8):
                per_row = jnp.where(row == j, own - occ[n, side * 8 + j], per_row)
            both = vir_rows[pl.ds(n, 1), :]
            both = jnp.broadcast_to(jnp.concatenate((both, both), axis=1), (8, 128))
            for pair in range(8):
                per_lane = both - jnp.where(lane < 64, occ[n, 2 * pair], occ[n, 2 * pair + 1])
                scale[side, n, :, pl.ds(pair * 128, 128)] = 1.0 / (per_row + per_lane)
            return 0

        lax.fori_loop(0, 16, per_block, 0)

    def pick(q, source, depth=1024):
        def per_block(n, _):
            picked[q, pl.ds(pl.multiple_of(n * 16, 16), 16), pl.ds(0, depth)] = source[partner[q, n]]
            return 0

        lax.fori_loop(0, 16, per_block, 0)

    def own_cycle(chunk):
        pick(0, strips[chunk])

        def columns(step, _):
            span = pl.ds(pl.multiple_of(step * 512, 512), 512)
            for part in range(2):
                total[chunk % 2, part, :, span] = jnp.dot(picked[0], w_ref[0, part, :, span], preferred_element_type=F32)
            return 0

        lax.fori_loop(0, 2, columns, 0)
        make_scale(chunk)

    def await_shifts(chunk, half):
        for copy in shifts(chunk, half):
            copy.wait_recv()

    def last_chunk_ahead():
        await_shifts(3, 0)
        pick(1, low_ref[3][0], CUT)
        pick(2, high_ref[3][0], CUT)

        def columns(step, _):
            span = pl.ds(pl.multiple_of(step * 512, 512), 512)
            for part in range(2):
                some = total[1, part, :, span]
                for q in (1, 2):
                    some += jnp.dot(
                        picked[q, :, :CUT], w_ref[q, part, pl.ds(0, CUT), span], preferred_element_type=F32
                    )
                total[1, part, :, span] = some
            return 0

        lax.fori_loop(0, 2, columns, 0)

    def far_cycle(chunk):
        if chunk == 3:
            start, depth = CUT, 1024 - CUT
            sources = low_ref[3][1], high_ref[3][1]
        else:
            await_shifts(chunk, 0)
            start, depth = 0, 1024
            sources = low_ref[chunk], high_ref[chunk]
        await_shifts(chunk, 1)
        for q in (1, 2):
            pick(q, sources[q - 1], depth)
        parity, side = chunk // 2, chunk % 2
        for step in range(2):
            span = pl.ds(step * 512, 512)
            sums = []
            for part in range(2):
                some = total[side, part, :, span]
                for q in (1, 2):
                    some += jnp.dot(
                        picked[q, :, :depth], w_ref[q, part, pl.ds(start, depth), span], preferred_element_type=F32
                    )
                sums.append(some.reshape(16, 2, 8, 512))
            by_real, by_imag = sums
            held = strips[chunk][:, :, span].astype(F32).reshape(16, 2, 8, 512)
            factor = scale[side, :, :, span]
            real = (held[:, 0] + (by_real[:, 0] - by_imag[:, 1])) * factor
            imag = (held[:, 1] + (by_imag[:, 0] + by_real[:, 1])) * factor
            result = jnp.stack((real, imag), axis=1).reshape(256, 512).astype(BF16)
            for n in range(16):
                half, place = n // 8, n % 8
                for pair in range(4):
                    regroup[pl.ds(half * 64 + pair * 16, 16), pl.ds(place * 128, 128)] = result[
                        n * 16 : (n + 1) * 16, pair * 128 : (pair + 1) * 128
                    ]
            for part in range(4):
                send2[parity, side, step, part // 2, pl.ds((part % 2) * 256, 256), :] = lax.dot_general(
                    two[pl.ds(part * 256, 256), :], regroup[...], NT, preferred_element_type=F32
                ).astype(BF16)
            where = parity, side, step
            y_ref[(*where, slice(None), mine)] = send2[(*where, slice(None), mine)]
            spread(send2.at[where], y_ref.at[where], send2_sem.at[where], recv2_sem.at[where])

    def store(step):
        span = pl.ds(step * 128, 128)
        return pltpu.make_async_copy(out.at[:, :, span], out_hbm.at[:, :, span], load_sem.at[5 + step])

    def unpacked(chunk, step):
        where = chunk // 2, chunk % 2, step
        await_peers(y_ref.at[where], recv2_sem.at[where])
        rows = jnp.concatenate([y_ref[(*where, low)].T for low in range(2)], axis=0)
        moved = jnp.dot(rows, one[pl.ds(where[0] * 512, 512), :], preferred_element_type=F32)
        return moved.reshape(2, 2, 4, 2, 8, 1024)

    def finish(chunks):
        for step in range(2):
            known = {chunk % 2: unpacked(chunk, step) for chunk in chunks}
            for place in range(8):
                for low in range(2):
                    for half in range(2):
                        for i in range(4):
                            for p in range(2):
                                tiles = [
                                    known[side][low, half, i, p, :, place * 128 : (place + 1) * 128]
                                    if side in known
                                    else jnp.zeros((8, 128), F32)
                                    for side in range(2)
                                ]
                                tile = jnp.concatenate(tiles, axis=0).astype(BF16)
                                spot = (half * 8 + place, p, pl.ds(((step * 4 + i) * 2 + low) * 16, 16))
                                out[spot] = tile if chunks[0] < 2 else out[spot] + tile
            if 3 in chunks:
                store(step).start()

    permutation(one, True)
    for copy in loads[0]:
        copy.wait()
    dress(0)
    arrange(0, 0)
    pl.semaphore_wait(barrier, RANKS + 1)
    spread_dressed(0, 0, 0)
    spread_dressed(0, 0, 1)
    for copy in loads[1]:
        copy.wait()
    dress(1)
    arrange(0, 1)
    permutation(two, False)
    await_dressed(0, 0, 0)
    make_strips(0, 0, (0,))
    start_shifts(0, 0)
    await_dressed(0, 0, 1)
    spread_dressed(0, 1, 0)
    spread_dressed(0, 1, 1)
    make_strips(0, 0, (1,))
    start_shifts(1, 0)
    arrange(1, 0)
    arrange(1, 1)

    def strips_both(parity, half):
        for side in range(2):
            await_dressed(parity, half, side)
        if (parity, half) != (1, 1):
            spread_dressed(1, parity, 0)
            spread_dressed(1, parity, 1)
        make_strips(parity, half, (0, 1))

    strips_both(0, 1)
    start_shifts(0, 1)
    start_shifts(1, 1)
    w_load.wait()
    for copy in small:
        copy.wait()
    own_cycle(0)
    own_cycle(1)
    strips_both(1, 0)
    start_shifts(2, 0)
    far_cycle(0)
    strips_both(1, 1)
    start_shifts(2, 1)
    start_shifts(3, 0)
    start_shifts(3, 1)
    far_cycle(1)
    own_cycle(2)
    own_cycle(3)
    far_cycle(2)
    finish((0, 1))
    last_chunk_ahead()
    far_cycle(3)
    finish((2,))
    finish((3,))
    for first in range(2):
        for second in range(2):
            for third in range(2):
                await_peers(send1.at[first, second, third], send1_sem.at[first, second, third])
                await_peers(send2.at[first, second, third], send2_sem.at[first, second, third])
    for chunk in range(4):
        for half in range(2):
            for copy in shifts(chunk, half):
                copy.wait_send()
    for half in range(2):
        store(half).wait()


def per_device(amplitudes, ladder, cycle, partner, occ_energy, vir_energy):
    hbm = pl.BlockSpec(memory_space=pltpu.HBM)
    exchanged = pltpu.VMEM((2, 2, 2, 2, 512, 128), BF16)
    field = pltpu.VMEM((16, 16, 1024), BF16)
    split = [pltpu.VMEM((16, 16, depth), BF16) for depth in (CUT, 1024 - CUT)]
    square = pltpu.VMEM((1024, 1024), BF16)
    dma = pltpu.SemaphoreType.DMA
    return pl.pallas_call(
        kernel,
        out_shape=jax.ShapeDtypeStruct((16, 2, 256, 128), BF16),
        in_specs=[hbm] * 6,
        out_specs=pl.BlockSpec(memory_space=pl.ANY),
        scratch_shapes=[
            pltpu.VMEM((16, 2, 256, 128), BF16),
            pltpu.VMEM((16, 2, 256, 256), BF16),
            pltpu.VMEM((3, 2, 1024, 1024), BF16),
            square,
            square,
            pltpu.VMEM((2, 2, 256, 1024), BF16),
            exchanged,
            exchanged,
            *[field] * 4,
            *([field] * 3 + split) * 2,
            pltpu.VMEM((3, 256, 1024), BF16),
            pltpu.VMEM((2, 2, 256, 1024), F32),
            pltpu.VMEM((2, 16, 8, 1024), F32),
            pltpu.VMEM((128, 1024), BF16),
            pltpu.VMEM((16, 2, 256, 128), BF16),
            pltpu.SMEM((3, 16), jnp.int32),
            pltpu.SMEM((16, 16), F32),
            pltpu.SMEM((16, 64), F32),
            pltpu.VMEM((16, 64), F32),
            exchanged,
            exchanged,
            dma((11,)),
            dma((2, 2, 2)),
            dma((2, 2, 2)),
            dma((2, 4, 2)),
            dma((2, 4, 2)),
            dma((2, 2, 2)),
            dma((2, 2, 2)),
        ],
        compiler_params=pltpu.CompilerParams(
            collective_id=0, has_side_effects=True, vmem_limit_bytes=60 * 1024 * 1024
        ),
    )(amplitudes, ladder, cycle[0], partner.T, occ_energy, vir_energy)


def solution(mesh):
    return jax.shard_map(
        per_device,
        mesh=mesh,
        in_specs=(
            P("kgrp", None, None, "vpair"),
            P("kgrp", None, None, None),
            P("kgrp", None, None, None, None),
            P("kgrp", None),
            P("kgrp", None),
            P("kgrp", None),
        ),
        out_specs=P("kgrp", None, None, "vpair"),
        check_vma=False,
    )
```

```python
import jax
import jax.numpy as jnp
from jax import lax
from jax.experimental import pallas as pl
from jax.experimental.pallas import tpu as pltpu
from jax.sharding import PartitionSpec as P

F32 = jnp.float32
BF16 = jnp.bfloat16
NT = (((1,), (1,)), ((), ()))
MESH = pl.DeviceIdType.MESH
RANKS = 32
STRIDE = 1
CUT = 768


def permutation(ref, swapped):
    def block(step, _):
        row = lax.broadcasted_iota(jnp.int32, (64, 1024), 0) + step * 64
        col = lax.broadcasted_iota(jnp.int32, (64, 1024), 1)
        x, r, n, y = row >> 9, (row >> 4) & 31, (row >> 1) & 7, row & 1
        if swapped:
            x, y = y, x
        target = n * 128 + x * 64 + r * 2 + y
        ref[pl.ds(pl.multiple_of(step * 64, 64), 64), :] = jnp.where(col == target, 1.0, 0.0).astype(BF16)
        return 0

    lax.fori_loop(0, 16, block, 0)


def kernel(
    t_hbm,
    l_hbm,
    w_hbm,
    partner_hbm,
    occ_hbm,
    vir_hbm,
    out_hbm,
    t_ref,
    l_ref,
    w_ref,
    one,
    two,
    dcat,
    send1,
    x_ref,
    *rest,
):
    strips, low_ref, high_ref = rest[:4], (*rest[4:7], rest[7:9]), (*rest[9:12], rest[12:14])
    (
        picked,
        total,
        scale,
        regroup,
        out,
        partner,
        occ,
        vir,
        vir_rows,
        send2,
        y_ref,
        load_sem,
        send1_sem,
        recv1_sem,
        shift_send_sem,
        shift_recv_sem,
        send2_sem,
        recv2_sem,
    ) = rest[14:]
    group = lax.axis_index("kgrp")
    me = lax.axis_index("vpair")
    above, below = lax.rem(group + 1, 4), lax.rem(group + 3, 4)

    barrier = pltpu.get_barrier_semaphore()
    mine_x, mine_y, mine_core = me // 8, (me // 2) % 4, me % 2

    def peer_of(i):
        turn = lax.rem(i * STRIDE, RANKS)
        x = lax.rem(mine_x + turn // 8, 4)
        y = lax.rem(mine_y + lax.rem(turn // 2, 4), 4)
        return x * 8 + y * 2 + lax.rem(mine_core + turn, 2)

    def greet(i, _):
        pl.semaphore_signal(barrier, inc=1, device_id=(group, peer_of(i)), device_id_type=MESH)
        return 0

    lax.fori_loop(1, RANKS, greet, 0)
    for other in (above, below):
        pl.semaphore_signal(barrier, inc=1, device_id=(other, me), device_id_type=MESH)

    loads = []
    for half in range(2):
        span = pl.ds(half * 8, 8)
        loads.append(
            (
                pltpu.make_async_copy(t_hbm.at[span], t_ref.at[span], load_sem.at[2 * half]),
                pltpu.make_async_copy(l_hbm.at[span], l_ref.at[span], load_sem.at[2 * half + 1]),
            )
        )
    small = [
        pltpu.make_async_copy(source, target, load_sem.at[7 + at])
        for at, (source, target) in enumerate(
            ((partner_hbm, partner), (occ_hbm, occ), (vir_hbm, vir), (vir_hbm, vir_rows))
        )
    ]
    w_load = pltpu.make_async_copy(w_hbm, w_ref, load_sem.at[4])
    for pair in loads:
        for copy in pair:
            copy.start()
    for copy in small:
        copy.start()
    w_load.start()

    mine = pl.ds(pl.multiple_of(me * 16, 16), 16)

    def spread(source, target, send_sem, recv_sem):
        ahead = (slice(None),) * (len(source.shape) - 2)

        def one_peer(i, _):
            peer = peer_of(i)
            pltpu.make_async_remote_copy(
                src_ref=source.at[(*ahead, pl.ds(pl.multiple_of(peer * 16, 16), 16), slice(None))],
                dst_ref=target.at[(*ahead, mine, slice(None))],
                send_sem=send_sem,
                recv_sem=recv_sem,
                device_id=(group, peer),
                device_id_type=MESH,
            ).start()
            return 0

        lax.fori_loop(1, RANKS, one_peer, 0)

    def await_peers(ref, sem):
        ahead = (slice(None),) * (len(ref.shape) - 2)
        part = ref.at[(*ahead, pl.ds(0, 16 * (RANKS - 1)), slice(None))]
        pltpu.make_async_copy(part, part, sem).wait()

    def dress(half):
        def per_block(place, _):
            n = half * 8 + place
            weights = jnp.concatenate((t_ref[n, 0], t_ref[n, 1]), axis=1)
            real = jnp.dot(l_ref[n, 0], weights, preferred_element_type=F32)
            imag = jnp.dot(l_ref[n, 1], weights, preferred_element_type=F32)
            lanes = pl.ds(pl.multiple_of(place * 128, 128), 128)
            parts = (real[:, :128] - imag[:, 128:], real[:, 128:] + imag[:, :128])
            parts = [part.reshape(8, 2, 2, 8, 128) for part in parts]
            for side in range(2):
                for low in range(2):
                    both = jnp.stack([part[:, low, side] for part in parts], axis=1)
                    dcat[side, half, pl.ds(low * 128, 128), lanes] = both.reshape(128, 128).astype(BF16)
            return 0

        lax.fori_loop(0, 8, per_block, 0)

    def arrange(parity, half):
        for side in range(2):
            for part in range(2):
                moved = lax.dot_general(
                    one[pl.ds(parity * 512 + part * 256, 256), :],
                    dcat[side, half],
                    NT,
                    preferred_element_type=F32,
                ).astype(BF16)
                for low in range(2):
                    send1[parity, half, side, low, pl.ds(part * 256, 256), :] = moved[:, low * 128 : (low + 1) * 128]
        x_ref[parity, half, :, :, mine, :] = send1[parity, half, :, :, mine, :]

    def spread_dressed(*where):
        spread(send1.at[where], x_ref.at[where], send1_sem.at[where], recv1_sem.at[where])

    def await_dressed(*where):
        await_peers(x_ref.at[where], recv1_sem.at[where])

    def shifts(chunk, half):
        if chunk == 3:
            source = strips[3].at[:, :, pl.ds(CUT * half, CUT + half * (1024 - 2 * CUT))]
        else:
            source = strips[chunk].at[pl.ds(half * 8, 8)]
        return [
            pltpu.make_async_remote_copy(
                src_ref=source,
                dst_ref=target[3][half] if chunk == 3 else target[chunk].at[pl.ds(half * 8, 8)],
                send_sem=shift_send_sem.at[way, chunk, half],
                recv_sem=shift_recv_sem.at[way, chunk, half],
                device_id=(other, me),
                device_id_type=MESH,
            )
            for way, (target, other) in enumerate(((low_ref, above), (high_ref, below)))
        ]

    def start_shifts(chunk, half):
        for copy in shifts(chunk, half):
            copy.start()

    def make_strips(parity, half, sides):
        rows = jnp.concatenate([x_ref[parity, half, side].reshape(1024, 128).T for side in sides], axis=0)
        moved = jnp.dot(rows, two[...], preferred_element_type=F32).astype(BF16)
        for at, side in enumerate(sides):
            for place in range(8):
                for k in range(8):
                    strips[2 * parity + side][half * 8 + place, :, pl.ds(k * 128, 128)] = moved[
                        at * 128 + k * 16 : at * 128 + (k + 1) * 16, place * 128 : (place + 1) * 128
                    ]

    def make_scale(chunk):
        parity, side = chunk // 2, chunk % 2

        def per_block(n, _):
            row = lax.broadcasted_iota(jnp.int32, (8, 128), 0)
            lane = lax.broadcasted_iota(jnp.int32, (8, 128), 1)
            own = vir[n, 2 * me + parity]
            per_row = jnp.zeros((8, 128), F32)
            for j in range(8):
                per_row = jnp.where(row == j, own - occ[n, side * 8 + j], per_row)
            both = vir_rows[pl.ds(n, 1), :]
            both = jnp.broadcast_to(jnp.concatenate((both, both), axis=1), (8, 128))
            for pair in range(8):
                per_lane = both - jnp.where(lane < 64, occ[n, 2 * pair], occ[n, 2 * pair + 1])
                scale[side, n, :, pl.ds(pair * 128, 128)] = 1.0 / (per_row + per_lane)
            return 0

        lax.fori_loop(0, 16, per_block, 0)

    def pick(q, source, depth=1024):
        def per_block(n, _):
            picked[q, pl.ds(pl.multiple_of(n * 16, 16), 16), pl.ds(0, depth)] = source[partner[q, n]]
            return 0

        lax.fori_loop(0, 16, per_block, 0)

    def own_cycle(chunk):
        pick(0, strips[chunk])

        def columns(step, _):
            span = pl.ds(pl.multiple_of(step * 512, 512), 512)
            for part in range(2):
                total[chunk % 2, part, :, span] = jnp.dot(picked[0], w_ref[0, part, :, span], preferred_element_type=F32)
            return 0

        lax.fori_loop(0, 2, columns, 0)
        make_scale(chunk)

    def await_shifts(chunk, half):
        for copy in shifts(chunk, half):
            copy.wait_recv()

    def last_chunk_ahead():
        await_shifts(3, 0)
        pick(1, low_ref[3][0], CUT)
        pick(2, high_ref[3][0], CUT)

        def columns(step, _):
            span = pl.ds(pl.multiple_of(step * 512, 512), 512)
            for part in range(2):
                some = total[1, part, :, span]
                for q in (1, 2):
                    some += jnp.dot(
                        picked[q, :, :CUT], w_ref[q, part, pl.ds(0, CUT), span], preferred_element_type=F32
                    )
                total[1, part, :, span] = some
            return 0

        lax.fori_loop(0, 2, columns, 0)

    def far_cycle(chunk):
        if chunk == 3:
            start, depth = CUT, 1024 - CUT
            sources = low_ref[3][1], high_ref[3][1]
        else:
            await_shifts(chunk, 0)
            start, depth = 0, 1024
            sources = low_ref[chunk], high_ref[chunk]
        await_shifts(chunk, 1)
        for q in (1, 2):
            pick(q, sources[q - 1], depth)
        parity, side = chunk // 2, chunk % 2
        for step in range(2):
            span = pl.ds(step * 512, 512)
            sums = []
            for part in range(2):
                some = total[side, part, :, span]
                for q in (1, 2):
                    some += jnp.dot(
                        picked[q, :, :depth], w_ref[q, part, pl.ds(start, depth), span], preferred_element_type=F32
                    )
                sums.append(some.reshape(16, 2, 8, 512))
            by_real, by_imag = sums
            held = strips[chunk][:, :, span].astype(F32).reshape(16, 2, 8, 512)
            factor = scale[side, :, :, span]
            real = (held[:, 0] + (by_real[:, 0] - by_imag[:, 1])) * factor
            imag = (held[:, 1] + (by_imag[:, 0] + by_real[:, 1])) * factor
            result = jnp.stack((real, imag), axis=1).reshape(256, 512).astype(BF16)
            for n in range(16):
                half, place = n // 8, n % 8
                for pair in range(4):
                    regroup[pl.ds(half * 64 + pair * 16, 16), pl.ds(place * 128, 128)] = result[
                        n * 16 : (n + 1) * 16, pair * 128 : (pair + 1) * 128
                    ]
            for part in range(4):
                send2[parity, side, step, part // 2, pl.ds((part % 2) * 256, 256), :] = lax.dot_general(
                    two[pl.ds(part * 256, 256), :], regroup[...], NT, preferred_element_type=F32
                ).astype(BF16)
            where = parity, side, step
            y_ref[(*where, slice(None), mine)] = send2[(*where, slice(None), mine)]
            spread(send2.at[where], y_ref.at[where], send2_sem.at[where], recv2_sem.at[where])

    def store(step):
        span = pl.ds(step * 128, 128)
        return pltpu.make_async_copy(out.at[:, :, span], out_hbm.at[:, :, span], load_sem.at[5 + step])

    def unpacked(chunk, step):
        where = chunk // 2, chunk % 2, step
        await_peers(y_ref.at[where], recv2_sem.at[where])
        rows = jnp.concatenate([y_ref[(*where, low)].T for low in range(2)], axis=0)
        moved = jnp.dot(rows, one[pl.ds(where[0] * 512, 512), :], preferred_element_type=F32)
        return moved.reshape(2, 2, 4, 2, 8, 1024)

    def finish(chunks):
        for step in range(2):
            known = {chunk % 2: unpacked(chunk, step) for chunk in chunks}
            for place in range(8):
                for low in range(2):
                    for half in range(2):
                        for i in range(4):
                            for p in range(2):
                                tiles = [
                                    known[side][low, half, i, p, :, place * 128 : (place + 1) * 128]
                                    if side in known
                                    else jnp.zeros((8, 128), F32)
                                    for side in range(2)
                                ]
                                tile = jnp.concatenate(tiles, axis=0).astype(BF16)
                                spot = (half * 8 + place, p, pl.ds(((step * 4 + i) * 2 + low) * 16, 16))
                                out[spot] = tile if chunks[0] < 2 else out[spot] + tile
            if 3 in chunks:
                store(step).start()

    permutation(one, True)
    for copy in loads[0]:
        copy.wait()
    dress(0)
    arrange(0, 0)
    pl.semaphore_wait(barrier, RANKS + 1)
    spread_dressed(0, 0, 0)
    spread_dressed(0, 0, 1)
    for copy in loads[1]:
        copy.wait()
    dress(1)
    arrange(0, 1)
    permutation(two, False)
    await_dressed(0, 0, 0)
    spread_dressed(0, 1, 0)
    make_strips(0, 0, (0,))
    start_shifts(0, 0)
    await_dressed(0, 0, 1)
    spread_dressed(0, 1, 1)
    make_strips(0, 0, (1,))
    start_shifts(1, 0)
    arrange(1, 0)
    arrange(1, 1)

    def strips_both(parity, half):
        for side in range(2):
            await_dressed(parity, half, side)
            if (parity, half) != (1, 1):
                spread_dressed(1, parity, side)
        make_strips(parity, half, (0, 1))

    strips_both(0, 1)
    start_shifts(0, 1)
    start_shifts(1, 1)
    w_load.wait()
    for copy in small:
        copy.wait()
    own_cycle(0)
    own_cycle(1)
    strips_both(1, 0)
    start_shifts(2, 0)
    far_cycle(0)
    strips_both(1, 1)
    start_shifts(2, 1)
    start_shifts(3, 0)
    start_shifts(3, 1)
    far_cycle(1)
    own_cycle(2)
    own_cycle(3)
    far_cycle(2)
    finish((0, 1))
    last_chunk_ahead()
    far_cycle(3)
    finish((2,))
    finish((3,))
    for first in range(2):
        for second in range(2):
            for third in range(2):
                await_peers(send1.at[first, second, third], send1_sem.at[first, second, third])
                await_peers(send2.at[first, second, third], send2_sem.at[first, second, third])
    for chunk in range(4):
        for half in range(2):
            for copy in shifts(chunk, half):
                copy.wait_send()
    for half in range(2):
        store(half).wait()


def per_device(amplitudes, ladder, cycle, partner, occ_energy, vir_energy):
    hbm = pl.BlockSpec(memory_space=pltpu.HBM)
    exchanged = pltpu.VMEM((2, 2, 2, 2, 512, 128), BF16)
    field = pltpu.VMEM((16, 16, 1024), BF16)
    split = [pltpu.VMEM((16, 16, depth), BF16) for depth in (CUT, 1024 - CUT)]
    square = pltpu.VMEM((1024, 1024), BF16)
    dma = pltpu.SemaphoreType.DMA
    return pl.pallas_call(
        kernel,
        out_shape=jax.ShapeDtypeStruct((16, 2, 256, 128), BF16),
        in_specs=[hbm] * 6,
        out_specs=pl.BlockSpec(memory_space=pl.ANY),
        scratch_shapes=[
            pltpu.VMEM((16, 2, 256, 128), BF16),
            pltpu.VMEM((16, 2, 256, 256), BF16),
            pltpu.VMEM((3, 2, 1024, 1024), BF16),
            square,
            square,
            pltpu.VMEM((2, 2, 256, 1024), BF16),
            exchanged,
            exchanged,
            *[field] * 4,
            *([field] * 3 + split) * 2,
            pltpu.VMEM((3, 256, 1024), BF16),
            pltpu.VMEM((2, 2, 256, 1024), F32),
            pltpu.VMEM((2, 16, 8, 1024), F32),
            pltpu.VMEM((128, 1024), BF16),
            pltpu.VMEM((16, 2, 256, 128), BF16),
            pltpu.SMEM((3, 16), jnp.int32),
            pltpu.SMEM((16, 16), F32),
            pltpu.SMEM((16, 64), F32),
            pltpu.VMEM((16, 64), F32),
            exchanged,
            exchanged,
            dma((11,)),
            dma((2, 2, 2)),
            dma((2, 2, 2)),
            dma((2, 4, 2)),
            dma((2, 4, 2)),
            dma((2, 2, 2)),
            dma((2, 2, 2)),
        ],
        compiler_params=pltpu.CompilerParams(
            collective_id=0, has_side_effects=True, vmem_limit_bytes=60 * 1024 * 1024
        ),
    )(amplitudes, ladder, cycle[0], partner.T, occ_energy, vir_energy)


def solution(mesh):
    return jax.shard_map(
        per_device,
        mesh=mesh,
        in_specs=(
            P("kgrp", None, None, "vpair"),
            P("kgrp", None, None, None),
            P("kgrp", None, None, None, None),
            P("kgrp", None),
            P("kgrp", None),
            P("kgrp", None),
        ),
        out_specs=P("kgrp", None, None, "vpair"),
        check_vma=False,
    )
```

```python
import jax
import jax.numpy as jnp
from jax import lax
from jax.experimental import pallas as pl
from jax.experimental.pallas import tpu as pltpu
from jax.sharding import PartitionSpec as P

F32 = jnp.float32
BF16 = jnp.bfloat16
NT = (((1,), (1,)), ((), ()))
MESH = pl.DeviceIdType.MESH
RANKS = 32
STRIDE = 1
CUT = 768


def permutation(ref, swapped):
    def block(step, _):
        row = lax.broadcasted_iota(jnp.int32, (64, 1024), 0) + step * 64
        col = lax.broadcasted_iota(jnp.int32, (64, 1024), 1)
        x, r, n, y = row >> 9, (row >> 4) & 31, (row >> 1) & 7, row & 1
        if swapped:
            x, y = y, x
        target = n * 128 + x * 64 + r * 2 + y
        ref[pl.ds(pl.multiple_of(step * 64, 64), 64), :] = jnp.where(col == target, 1.0, 0.0).astype(BF16)
        return 0

    lax.fori_loop(0, 16, block, 0)


def kernel(
    t_hbm,
    l_hbm,
    w_hbm,
    partner_hbm,
    occ_hbm,
    vir_hbm,
    out_hbm,
    t_ref,
    l_ref,
    w_ref,
    one,
    two,
    dcat,
    send1,
    x_ref,
    *rest,
):
    strips, low_ref, high_ref = rest[:4], (*rest[4:7], rest[7:9]), (*rest[9:12], rest[12:14])
    (
        picked,
        total,
        scale,
        regroup,
        out,
        partner,
        occ,
        vir,
        vir_rows,
        send2,
        y_ref,
        load_sem,
        send1_sem,
        recv1_sem,
        shift_send_sem,
        shift_recv_sem,
        send2_sem,
        recv2_sem,
    ) = rest[14:]
    group = lax.axis_index("kgrp")
    me = lax.axis_index("vpair")
    above, below = lax.rem(group + 1, 4), lax.rem(group + 3, 4)

    barrier = pltpu.get_barrier_semaphore()
    mine_x, mine_y, mine_core = me // 8, (me // 2) % 4, me % 2

    def peer_of(i):
        turn = lax.rem(i * STRIDE, RANKS)
        x = lax.rem(mine_x + turn // 8, 4)
        y = lax.rem(mine_y + lax.rem(turn // 2, 4), 4)
        return x * 8 + y * 2 + lax.rem(mine_core + turn, 2)

    def greet(i, _):
        pl.semaphore_signal(barrier, inc=1, device_id=(group, peer_of(i)), device_id_type=MESH)
        return 0

    lax.fori_loop(1, RANKS, greet, 0)
    for other in (above, below):
        pl.semaphore_signal(barrier, inc=1, device_id=(other, me), device_id_type=MESH)

    loads = []
    for half in range(2):
        span = pl.ds(half * 8, 8)
        loads.append(
            (
                pltpu.make_async_copy(t_hbm.at[span], t_ref.at[span], load_sem.at[2 * half]),
                pltpu.make_async_copy(l_hbm.at[span], l_ref.at[span], load_sem.at[2 * half + 1]),
            )
        )
    small = [
        pltpu.make_async_copy(source, target, load_sem.at[7 + at])
        for at, (source, target) in enumerate(
            ((partner_hbm, partner), (occ_hbm, occ), (vir_hbm, vir), (vir_hbm, vir_rows))
        )
    ]
    w_load = pltpu.make_async_copy(w_hbm, w_ref, load_sem.at[4])
    for pair in loads:
        for copy in pair:
            copy.start()
    for copy in small:
        copy.start()
    w_load.start()

    mine = pl.ds(pl.multiple_of(me * 16, 16), 16)

    def spread(source, target, send_sem, recv_sem):
        ahead = (slice(None),) * (len(source.shape) - 2)

        def one_peer(i, _):
            peer = peer_of(i)
            pltpu.make_async_remote_copy(
                src_ref=source.at[(*ahead, pl.ds(pl.multiple_of(peer * 16, 16), 16), slice(None))],
                dst_ref=target.at[(*ahead, mine, slice(None))],
                send_sem=send_sem,
                recv_sem=recv_sem,
                device_id=(group, peer),
                device_id_type=MESH,
            ).start()
            return 0

        lax.fori_loop(1, RANKS, one_peer, 0)

    def await_peers(ref, sem):
        ahead = (slice(None),) * (len(ref.shape) - 2)
        part = ref.at[(*ahead, pl.ds(0, 16 * (RANKS - 1)), slice(None))]
        pltpu.make_async_copy(part, part, sem).wait()

    def dress(half):
        def per_block(place, _):
            n = half * 8 + place
            weights = jnp.concatenate((t_ref[n, 0], t_ref[n, 1]), axis=1)
            real = jnp.dot(l_ref[n, 0], weights, preferred_element_type=F32)
            imag = jnp.dot(l_ref[n, 1], weights, preferred_element_type=F32)
            lanes = pl.ds(pl.multiple_of(place * 128, 128), 128)
            parts = (real[:, :128] - imag[:, 128:], real[:, 128:] + imag[:, :128])
            parts = [part.reshape(8, 2, 2, 8, 128) for part in parts]
            for side in range(2):
                for low in range(2):
                    both = jnp.stack([part[:, low, side] for part in parts], axis=1)
                    dcat[side, half, pl.ds(low * 128, 128), lanes] = both.reshape(128, 128).astype(BF16)
            return 0

        lax.fori_loop(0, 8, per_block, 0)

    def arrange(parity, half):
        for side in range(2):
            for part in range(2):
                moved = lax.dot_general(
                    one[pl.ds(parity * 512 + part * 256, 256), :],
                    dcat[side, half],
                    NT,
                    preferred_element_type=F32,
                ).astype(BF16)
                for low in range(2):
                    send1[parity, half, side, low, pl.ds(part * 256, 256), :] = moved[:, low * 128 : (low + 1) * 128]
        x_ref[parity, half, :, :, mine, :] = send1[parity, half, :, :, mine, :]

    def spread_dressed(*where):
        spread(send1.at[where], x_ref.at[where], send1_sem.at[where], recv1_sem.at[where])

    def await_dressed(*where):
        await_peers(x_ref.at[where], recv1_sem.at[where])

    def shifts(chunk, half):
        if chunk == 3:
            source = strips[3].at[:, :, pl.ds(CUT * half, CUT + half * (1024 - 2 * CUT))]
        else:
            source = strips[chunk].at[pl.ds(half * 8, 8)]
        return [
            pltpu.make_async_remote_copy(
                src_ref=source,
                dst_ref=target[3][half] if chunk == 3 else target[chunk].at[pl.ds(half * 8, 8)],
                send_sem=shift_send_sem.at[way, chunk, half],
                recv_sem=shift_recv_sem.at[way, chunk, half],
                device_id=(other, me),
                device_id_type=MESH,
            )
            for way, (target, other) in enumerate(((low_ref, above), (high_ref, below)))
        ]

    def start_shifts(chunk, half):
        for copy in shifts(chunk, half):
            copy.start()

    def make_strips(parity, half, sides):
        rows = jnp.concatenate([x_ref[parity, half, side].reshape(1024, 128).T for side in sides], axis=0)
        moved = jnp.dot(rows, two[...], preferred_element_type=F32).astype(BF16)
        for at, side in enumerate(sides):
            for place in range(8):
                for k in range(8):
                    strips[2 * parity + side][half * 8 + place, :, pl.ds(k * 128, 128)] = moved[
                        at * 128 + k * 16 : at * 128 + (k + 1) * 16, place * 128 : (place + 1) * 128
                    ]

    def make_scale(chunk):
        parity, side = chunk // 2, chunk % 2

        def per_block(n, _):
            row = lax.broadcasted_iota(jnp.int32, (8, 128), 0)
            lane = lax.broadcasted_iota(jnp.int32, (8, 128), 1)
            own = vir[n, 2 * me + parity]
            per_row = jnp.zeros((8, 128), F32)
            for j in range(8):
                per_row = jnp.where(row == j, own - occ[n, side * 8 + j], per_row)
            both = vir_rows[pl.ds(n, 1), :]
            both = jnp.broadcast_to(jnp.concatenate((both, both), axis=1), (8, 128))
            for pair in range(8):
                per_lane = both - jnp.where(lane < 64, occ[n, 2 * pair], occ[n, 2 * pair + 1])
                scale[side, n, :, pl.ds(pair * 128, 128)] = 1.0 / (per_row + per_lane)
            return 0

        lax.fori_loop(0, 16, per_block, 0)

    def pick(q, source, depth=1024):
        def per_block(n, _):
            picked[q, pl.ds(pl.multiple_of(n * 16, 16), 16), pl.ds(0, depth)] = source[partner[q, n]]
            return 0

        lax.fori_loop(0, 16, per_block, 0)

    def own_cycle(chunk):
        pick(0, strips[chunk])

        def columns(step, _):
            span = pl.ds(pl.multiple_of(step * 512, 512), 512)
            for part in range(2):
                total[chunk % 2, part, :, span] = jnp.dot(picked[0], w_ref[0, part, :, span], preferred_element_type=F32)
            return 0

        lax.fori_loop(0, 2, columns, 0)
        make_scale(chunk)

    def await_shifts(chunk, half):
        for copy in shifts(chunk, half):
            copy.wait_recv()

    def last_chunk_ahead():
        await_shifts(3, 0)
        pick(1, low_ref[3][0], CUT)
        pick(2, high_ref[3][0], CUT)

        def columns(step, _):
            span = pl.ds(pl.multiple_of(step * 512, 512), 512)
            for part in range(2):
                some = total[1, part, :, span]
                for q in (1, 2):
                    some += jnp.dot(
                        picked[q, :, :CUT], w_ref[q, part, pl.ds(0, CUT), span], preferred_element_type=F32
                    )
                total[1, part, :, span] = some
            return 0

        lax.fori_loop(0, 2, columns, 0)

    def far_cycle(chunk):
        if chunk == 3:
            start, depth = CUT, 1024 - CUT
            sources = low_ref[3][1], high_ref[3][1]
        else:
            await_shifts(chunk, 0)
            start, depth = 0, 1024
            sources = low_ref[chunk], high_ref[chunk]
        await_shifts(chunk, 1)
        for q in (1, 2):
            pick(q, sources[q - 1], depth)
        parity, side = chunk // 2, chunk % 2
        for step in range(2):
            span = pl.ds(step * 512, 512)
            sums = []
            for part in range(2):
                some = total[side, part, :, span]
                for q in (1, 2):
                    some += jnp.dot(
                        picked[q, :, :depth], w_ref[q, part, pl.ds(start, depth), span], preferred_element_type=F32
                    )
                sums.append(some.reshape(16, 2, 8, 512))
            by_real, by_imag = sums
            held = strips[chunk][:, :, span].astype(F32).reshape(16, 2, 8, 512)
            factor = scale[side, :, :, span]
            real = (held[:, 0] + (by_real[:, 0] - by_imag[:, 1])) * factor
            imag = (held[:, 1] + (by_imag[:, 0] + by_real[:, 1])) * factor
            result = jnp.stack((real, imag), axis=1).reshape(256, 512).astype(BF16)
            for n in range(16):
                half, place = n // 8, n % 8
                for pair in range(4):
                    regroup[pl.ds(half * 64 + pair * 16, 16), pl.ds(place * 128, 128)] = result[
                        n * 16 : (n + 1) * 16, pair * 128 : (pair + 1) * 128
                    ]
            for part in range(4):
                send2[parity, side, step, part // 2, pl.ds((part % 2) * 256, 256), :] = lax.dot_general(
                    two[pl.ds(part * 256, 256), :], regroup[...], NT, preferred_element_type=F32
                ).astype(BF16)
            where = parity, side, step
            y_ref[(*where, slice(None), mine)] = send2[(*where, slice(None), mine)]
            spread(send2.at[where], y_ref.at[where], send2_sem.at[where], recv2_sem.at[where])

    def store(step):
        span = pl.ds(step * 128, 128)
        return pltpu.make_async_copy(out.at[:, :, span], out_hbm.at[:, :, span], load_sem.at[5 + step])

    def unpacked(chunk, step):
        where = chunk // 2, chunk % 2, step
        await_peers(y_ref.at[where], recv2_sem.at[where])
        rows = jnp.concatenate([y_ref[(*where, low)].T for low in range(2)], axis=0)
        moved = jnp.dot(rows, one[pl.ds(where[0] * 512, 512), :], preferred_element_type=F32)
        return moved.reshape(2, 2, 4, 2, 8, 1024)

    def finish(chunks):
        for step in range(2):
            known = {chunk % 2: unpacked(chunk, step) for chunk in chunks}
            for place in range(8):
                for low in range(2):
                    for half in range(2):
                        for i in range(4):
                            for p in range(2):
                                tiles = [
                                    known[side][low, half, i, p, :, place * 128 : (place + 1) * 128]
                                    if side in known
                                    else jnp.zeros((8, 128), F32)
                                    for side in range(2)
                                ]
                                tile = jnp.concatenate(tiles, axis=0).astype(BF16)
                                spot = (half * 8 + place, p, pl.ds(((step * 4 + i) * 2 + low) * 16, 16))
                                out[spot] = tile if chunks[0] < 2 else out[spot] + tile
            if 3 in chunks:
                store(step).start()

    permutation(one, True)
    for copy in loads[0]:
        copy.wait()
    dress(0)
    arrange(0, 0)
    pl.semaphore_wait(barrier, RANKS + 1)
    spread_dressed(0, 0, 0)
    spread_dressed(0, 0, 1)
    for copy in loads[1]:
        copy.wait()
    dress(1)
    arrange(0, 1)
    permutation(two, False)
    await_dressed(0, 0, 0)
    spread_dressed(0, 1, 0)
    make_strips(0, 0, (0,))
    start_shifts(0, 0)
    await_dressed(0, 0, 1)
    spread_dressed(0, 1, 1)
    make_strips(0, 0, (1,))
    start_shifts(1, 0)
    arrange(1, 0)
    arrange(1, 1)

    def strips_both(parity, half):
        for side in range(2):
            await_dressed(parity, half, side)
            if (parity, half) != (1, 1):
                spread_dressed(1, parity, side)
        make_strips(parity, half, (0, 1))

    strips_both(0, 1)
    start_shifts(0, 1)
    start_shifts(1, 1)
    w_load.wait()
    for copy in small:
        copy.wait()
    own_cycle(0)
    own_cycle(1)
    strips_both(1, 0)
    start_shifts(2, 0)
    far_cycle(0)
    strips_both(1, 1)
    start_shifts(2, 1)
    start_shifts(3, 0)
    start_shifts(3, 1)
    far_cycle(1)
    own_cycle(2)
    own_cycle(3)
    far_cycle(2)
    last_chunk_ahead()
    far_cycle(3)
    finish((0, 1))
    finish((2,))
    finish((3,))
    for first in range(2):
        for second in range(2):
            for third in range(2):
                await_peers(send1.at[first, second, third], send1_sem.at[first, second, third])
                await_peers(send2.at[first, second, third], send2_sem.at[first, second, third])
    for chunk in range(4):
        for half in range(2):
            for copy in shifts(chunk, half):
                copy.wait_send()
    for half in range(2):
        store(half).wait()


def per_device(amplitudes, ladder, cycle, partner, occ_energy, vir_energy):
    hbm = pl.BlockSpec(memory_space=pltpu.HBM)
    exchanged = pltpu.VMEM((2, 2, 2, 2, 512, 128), BF16)
    field = pltpu.VMEM((16, 16, 1024), BF16)
    split = [pltpu.VMEM((16, 16, depth), BF16) for depth in (CUT, 1024 - CUT)]
    square = pltpu.VMEM((1024, 1024), BF16)
    dma = pltpu.SemaphoreType.DMA
    return pl.pallas_call(
        kernel,
        out_shape=jax.ShapeDtypeStruct((16, 2, 256, 128), BF16),
        in_specs=[hbm] * 6,
        out_specs=pl.BlockSpec(memory_space=pl.ANY),
        scratch_shapes=[
            pltpu.VMEM((16, 2, 256, 128), BF16),
            pltpu.VMEM((16, 2, 256, 256), BF16),
            pltpu.VMEM((3, 2, 1024, 1024), BF16),
            square,
            square,
            pltpu.VMEM((2, 2, 256, 1024), BF16),
            exchanged,
            exchanged,
            *[field] * 4,
            *([field] * 3 + split) * 2,
            pltpu.VMEM((3, 256, 1024), BF16),
            pltpu.VMEM((2, 2, 256, 1024), F32),
            pltpu.VMEM((2, 16, 8, 1024), F32),
            pltpu.VMEM((128, 1024), BF16),
            pltpu.VMEM((16, 2, 256, 128), BF16),
            pltpu.SMEM((3, 16), jnp.int32),
            pltpu.SMEM((16, 16), F32),
            pltpu.SMEM((16, 64), F32),
            pltpu.VMEM((16, 64), F32),
            exchanged,
            exchanged,
            dma((11,)),
            dma((2, 2, 2)),
            dma((2, 2, 2)),
            dma((2, 4, 2)),
            dma((2, 4, 2)),
            dma((2, 2, 2)),
            dma((2, 2, 2)),
        ],
        compiler_params=pltpu.CompilerParams(
            collective_id=0, has_side_effects=True, vmem_limit_bytes=60 * 1024 * 1024
        ),
    )(amplitudes, ladder, cycle[0], partner.T, occ_energy, vir_energy)


def solution(mesh):
    return jax.shard_map(
        per_device,
        mesh=mesh,
        in_specs=(
            P("kgrp", None, None, "vpair"),
            P("kgrp", None, None, None),
            P("kgrp", None, None, None, None),
            P("kgrp", None),
            P("kgrp", None),
            P("kgrp", None),
        ),
        out_specs=P("kgrp", None, None, "vpair"),
        check_vma=False,
    )
```
